256 devices in a mesh: ep: 2 (over x_hi), row: 16 (over y, x_lo, core), col: 8 (over z).
Axes of the slice: x: 4 (x_hi: 2, x_lo: 2; x = x_hi * 2 + x_lo), y: 4, z: 8, core: 2. Of those that a mesh axis runs over, the one named last changes fastest.
Arguments:
- design: bfloat16 [1024, 16384], P(('ep', 'col'), 'row'), may hold values from -0.09375 to 0.09375
- taps: float32 [64], replicated, may hold values from -1 to 1
- tap_count: int32 [1024], P(('ep', 'col')), may hold values from 32 to 64
- order: int32 [16384], P('row'), may hold values from 0 to 16383, as said below
- regular: float32 [16384], replicated, may hold values from 0.5 to 2
Outputs:
- factored: float32 [16384, 16384], P('row', ('ep', 'col'))
The draws below stay inside these ranges and needn't reach their ends.
Inputs may be any that keep to these rules, and one draw needn't show every extreme that they name: `order`: a permutation of 0 to 16383 that maps every index into its own aligned group of 128.
All inputs are finite; a program needn't handle non-finite values.
Results may differ from the reference program's by a relative error of at most 0.0037.
Values may be sent and summed in bfloat16 or wider, within the bound.
A program may use at most 64 MiB of HBM per device.

```python
import math
import jax
import jax.numpy as jnp
from jax import lax

P_SIZE = 16384
PANEL = 256
PB = 128
TAPS = 64
E = 1024


def draw_order(key, part):
    group_keys = jax.random.split(key, P_SIZE // PB)
    group_perms = jax.vmap(lambda single: jax.random.permutation(single, PB))(group_keys)
    bases = jnp.arange(P_SIZE // PB, dtype=jnp.int32) * PB
    return (group_perms.astype(jnp.int32) + bases[:, None]).reshape(P_SIZE).astype(jnp.int32)


def plant(drawn, rng, low, largest):
    spot = [jax.random.randint(jax.random.fold_in(rng, axis), (), 0, length) for axis, length in enumerate(drawn.shape)]
    longest = drawn.shape.index(max(drawn.shape))
    neighbour = spot[:longest] + [(spot[longest] + 1) % drawn.shape[longest]] + spot[longest + 1:]
    return drawn.at[tuple(spot)].set(low).at[tuple(neighbour)].set(largest)


def level_of(stream_key, shape, cuts, low, largest):
    def one(position, parts):
        draws = jax.random.uniform(jax.random.fold_in(jax.random.fold_in(stream_key, 6), position), (parts,), jnp.float32, low / len(cuts), largest / len(cuts))
        return jnp.repeat(jnp.exp(draws), shape[position] // parts).reshape((-1,) + (1,) * (len(shape) - position - 1))

    factor_of = one(*cuts[0])
    for cut in cuts[1:]:
        factor_of = factor_of * one(*cut)
    return factor_of


def gaussian(key, dims, deviation, most, cuts=(), held_as=jnp.bfloat16):
    array = jax.random.normal(key, dims, jnp.float32) * deviation
    if len(cuts) > 0:
        array = level_of(key, dims, cuts, -0.22, 0.18) * array
    return jnp.clip(array, min=-most, max=most).astype(held_as)


def setup_inputs(seed: int = 0) -> dict:
    streams_of = jax.random.split(jax.random.key(seed), 6)
    design = gaussian(streams_of[0], (E, P_SIZE), (4 * E) ** -0.5, 0.09375, ((0, 16), (1, 16)))
    taps = gaussian(streams_of[1], (TAPS,), 0.25, 1.0, (), jnp.float32)
    tap_count = plant(jax.random.randint(streams_of[2], (E,), TAPS // 2, TAPS + 1), jax.random.fold_in(streams_of[2], 1), TAPS // 2, TAPS).astype(jnp.int32)
    order = draw_order(jax.random.fold_in(streams_of[5], 71), 0)
    regular = jnp.clip(jnp.exp(jax.random.uniform(streams_of[4], (P_SIZE,), jnp.float32, math.log(0.5), math.log(2.0))), 0.5, 2.0)
    return dict(design=design, taps=taps, tap_count=tap_count, order=order, regular=regular)


def reference(design, taps, tap_count, order, regular):
    epoch_out = jnp.arange(E, dtype=jnp.int32)[:, None]
    epoch_in = jnp.arange(E, dtype=jnp.int32)[None, :]
    lag_steps = epoch_out - epoch_in
    valid = (lag_steps >= 0) & (lag_steps < tap_count.astype(jnp.int32)[:, None])
    toeplitz = jnp.where(valid, taps[jnp.clip(lag_steps, 0, TAPS - 1)], jnp.zeros((), taps.dtype)).astype(jnp.bfloat16)
    filtered = jnp.dot(toeplitz.astype(jnp.float32), design.astype(jnp.float32), preferred_element_type=jnp.float32).astype(jnp.bfloat16)
    permuted = jnp.take(filtered, order.astype(jnp.int32), axis=1)
    normal = jnp.dot(permuted.T.astype(jnp.float32), permuted.astype(jnp.float32), preferred_element_type=jnp.float32)
    all_rows = jnp.arange(P_SIZE, dtype=jnp.int32)
    normal = normal + jnp.diag(regular.astype(normal.dtype))
    for section in range(2):
        start_col = section * PANEL
        end_col = start_col + PANEL
        factor = jnp.linalg.cholesky(normal[start_col:end_col, start_col:end_col])
        solved = jax.scipy.linalg.solve_triangular(factor, normal[:, start_col:end_col].T, lower=True).T
        panel_factor = jnp.where((all_rows >= start_col)[:, None], solved, jnp.zeros((), solved.dtype))
        update = normal[:, end_col:] - jnp.dot(panel_factor, panel_factor[end_col:].T, precision=lax.Precision.HIGHEST)
        update = jnp.where((all_rows >= end_col)[:, None], update, jnp.zeros((), update.dtype))
        normal = jnp.concatenate([normal[:, :start_col], panel_factor, update], axis=1)
    return normal
```

```python
import functools

import jax
import jax.numpy as jnp
from jax import lax
from jax.experimental import pallas as pl
from jax.experimental.pallas import tpu as pltpu
from jax.sharding import PartitionSpec as P

MESH = pl.DeviceIdType.MESH
F32 = jnp.float32
BF16 = jnp.bfloat16
HIGHEST = lax.Precision.HIGHEST
PB = 128
PAN = 512
EB = 64
NE = 16
HALF = 256


def dot_nn(a, b, precision=None):
    return lax.dot_general(
        a, b, (((1,), (0,)), ((), ())), precision=precision, preferred_element_type=F32
    )


def dot_nt(a, b, precision=None):
    return lax.dot_general(
        a, b, (((1,), (1,)), ((), ())), precision=precision, preferred_element_type=F32
    )


def split2(x):
    high = x.astype(BF16)
    return high, (x - high.astype(F32)).astype(BF16)


def lane_bcast(v, j):
    return jnp.broadcast_to(v[:, j : j + 1], (8, 128))


def row_bcast(v, k):
    return jnp.broadcast_to(v[k : k + 1, :], (8, 128))


def invert_factor(groups):
    sub = lax.broadcasted_iota(jnp.int32, (8, 128), 0)
    lane = lax.broadcasted_iota(jnp.int32, (8, 128), 1)
    a = list(groups)
    g = [jnp.where(lane == sub + 8 * q, 1.0, 0.0).astype(F32) for q in range(16)]
    for p in range(16):
        v = a[p]
        c = [lane_bcast(v, 8 * p + k) for k in range(8)]
        s = [[None] * 8 for _ in range(8)]
        for k in range(8):
            for i in range(k, 8):
                s[i][k] = row_bcast(c[k], i)
        rinv = [None] * 8
        lcol = [None] * 8
        dvec = None
        gp = g[p]
        for k in range(8):
            r = 1.0 / s[k][k]
            rinv[k] = r
            for i in range(k + 1, 8):
                m = s[i][k] * r
                for j in range(k + 1, i + 1):
                    s[i][j] = s[i][j] - m * s[j][k]
            if k < 7:
                lcol[k] = jnp.where(sub > k, c[k] * r, 0.0)
                for m in range(k + 1, 8):
                    c[m] = c[m] - lcol[k] * s[m][k]
            dvec = s[k][k] if dvec is None else jnp.where(sub == k, s[k][k], dvec)
        vrow = [None] * 8
        grow = [None] * 8
        for k in range(8):
            vrow[k] = row_bcast(v, k)
            grow[k] = row_bcast(gp, k)
            if k < 7:
                v = v - lcol[k] * vrow[k]
                gp = gp - lcol[k] * grow[k]
        for q in range(p + 1, 16):
            d = [lane_bcast(a[q], 8 * p + k) for k in range(8)]
            for k in range(8):
                d[k] = d[k] * rinv[k]
                for m in range(k + 1, 8):
                    d[m] = d[m] - d[k] * s[m][k]
            aq, gq = a[q], g[q]
            for k in range(8):
                aq = aq - d[k] * vrow[k]
                gq = gq - d[k] * grow[k]
            a[q], g[q] = aq, gq
        g[p] = gp * lax.rsqrt(dvec)
    return g


def factor_step(s, w, b):
    n = s.shape[0]
    lo, hi = 128 * b, 128 * b + 128
    g = invert_factor([s[lo + 8 * q : lo + 8 * q + 8, lo:hi] for q in range(16)])
    for q in range(16):
        w[lo + 8 * q : lo + 8 * q + 8, lo:hi] = g[q]
    inv = w[lo:hi, lo:hi]
    if b > 0:
        w[lo:hi, :lo] = dot_nn(inv, w[lo:hi, :lo], HIGHEST)
    if hi < n:
        below = dot_nt(s[hi:, lo:hi], inv, HIGHEST)
        s[hi:, hi:] = s[hi:, hi:] - dot_nt(below, below, HIGHEST)
        w[hi:, :hi] = w[hi:, :hi] - dot_nn(below, w[lo:hi, :hi], HIGHEST)


def gather_kernel(
    design_ref, taps_ref, count_ref, order_ref, reg_ref,
    frt_ref, fc_ref, rr_ref, rct_ref,
    xr, xc, rp, po, pf, pft, smat, wmat,
    bx_s, bx_r, br_s, br_r, p1_s, p1_r, c1_s, c1_r, xs, xq, rs, rq, c2_s, c2_r, cc_s, cc_r, cp_s, cp_r,
):
    ep = lax.axis_index("ep")
    row = lax.axis_index("row")
    col = lax.axis_index("col")
    core = row % 2
    e_own = ep * 8 + col
    group = e_own
    up, down = (col + 1) % 8, (col + 7) % 8
    to_up = {"ep": ep, "row": row, "col": up}
    to_down = {"ep": ep, "row": row, "col": down}
    to_ep = {"ep": 1 - ep, "row": row, "col": col}
    core_row = row - core + (1 - core)
    xlo = (row // 2) % 2
    x_row = row + 2 - 4 * xlo
    yup_row, ydown_row = (row + 4) % 16, (row + 12) % 16
    plane = lambda r: {"ep": ep, "row": r, "col": col}
    is_self = jnp.logical_and(row == group, core == ep)

    barrier = pltpu.get_barrier_semaphore()
    for dev in (to_up, to_down, to_ep, plane(core_row), plane(x_row), plane(yup_row), plane(ydown_row)):
        pl.semaphore_signal(barrier, inc=1, device_id=dev, device_id_type=MESH)

    @pl.when(row != 0)
    def _():
        pl.semaphore_signal(barrier, inc=1, device_id=plane(0), device_id_type=MESH)

    for z in range(8):
        mine = jnp.logical_and(is_self, col == z)

        @pl.when(jnp.logical_not(mine))
        def _():
            pl.semaphore_signal(
                barrier, inc=1, device_id={"ep": core, "row": group, "col": z}, device_id_type=MESH
            )

    local = order_ref[...] % PB
    kk = lax.broadcasted_iota(jnp.int32, (PB, 1024), 0)
    one_hot = jnp.where(kk == local, 1.0, 0.0).astype(BF16)
    own = e_own + 1
    for g in range(8):
        part = dot_nn(design_ref[:, g * PB : (g + 1) * PB], one_hot[:, g * PB : (g + 1) * PB])
        xr[own, :, g * PB : (g + 1) * PB] = part.astype(BF16)
    ii = lax.broadcasted_iota(jnp.int32, (EB, 128), 0)
    jj = lax.broadcasted_iota(jnp.int32, (EB, 128), 1)
    lag = ii + EB - jj
    ti = lax.broadcasted_iota(jnp.int32, (EB, EB), 0)
    tj = lax.broadcasted_iota(jnp.int32, (EB, EB), 1)
    counts = jnp.sum(jnp.where(ti == tj, count_ref[...].astype(F32), 0.0), axis=1, keepdims=True)
    band = jnp.zeros((EB, 128), F32)
    for t in range(taps_ref.shape[0]):
        band = jnp.where(lag == t, taps_ref[t], band)
    band = jnp.where(lag.astype(F32) < counts, band, 0.0)
    rp[own, :, HALF:] = band.astype(BF16)
    xr[0] = jnp.zeros(xr.shape[1:], BF16)
    rp[0] = jnp.zeros(rp.shape[1:], BF16)
    po[0] = jnp.zeros(po.shape[1:], BF16)
    for q in range(8):
        xc[q, 0] = jnp.zeros((EB, PB), BF16)

    @pl.when(row == 0)
    def _():
        rp[own, :, :HALF] = xr[own, :, :HALF]

    pl.semaphore_wait(
        barrier, 7 + 8 + jnp.where(row == 0, 15, 0) - jnp.where(is_self, 1, 0)
    )

    sends = []

    def remote(src, dst, s_sem, r_sem, dev):
        return pltpu.make_async_remote_copy(
            src_ref=src, dst_ref=dst, send_sem=s_sem, recv_sem=r_sem, device_id=dev, device_id_type=MESH
        )

    def send(src, dst, s_sem, r_sem, dev):
        copy = remote(src, dst, s_sem, r_sem, dev)
        copy.start()
        sends.append(copy)

    @pl.when(row == 0)
    def _():
        for t in range(1, 16):
            half = t % 2
            remote(
                xr.at[own, :, half * HALF : (half + 1) * HALF], rp.at[own, :, 0:HALF],
                p1_s.at[t - 1], p1_r, plane(t),
            ).start()

    eps = (ep, 1 - ep)

    def ring_origin(direction, s):
        return (col + 8 - s) % 8 if direction == 0 else (col + s) % 8

    def ring_piece(buf, k, z, direction, s):
        slot = eps[k] * 8 + z + 1
        if s < 3:
            return buf.at[slot]
        return buf.at[slot, pl.ds(32 * direction, 32)]

    def ring_send(buf, ssem, rsem, direction, s, k):
        piece = ring_piece(buf, k, ring_origin(direction, s), direction, s)
        send(piece, piece, ssem.at[direction, s, k], rsem.at[direction, s, k], (to_up, to_down)[direction])

    def ring_wait(buf, ssem, rsem, direction, s, k):
        piece = ring_piece(buf, k, ring_origin(direction, s + 1), direction, s)
        remote(piece, piece, ssem.at[direction, s, k], rsem.at[direction, s, k], to_up).wait_recv()

    for direction in range(2):
        ring_send(xr, xs, xq, direction, 0, 0)
    for q in range(8):
        src = xr.at[own, :, q * PB : (q + 1) * PB]
        dst = xc.at[q, own]
        mine = jnp.logical_and(is_self, row // 2 == q)

        @pl.when(jnp.logical_not(mine))
        def _():
            remote(
                src, dst, c1_s.at[q], c1_r.at[col],
                {"ep": row // 8, "row": 2 * q + ep, "col": row % 8},
            ).start()

        @pl.when(mine)
        def _():
            pltpu.make_async_copy(src, dst, c1_r.at[col]).start()

    @pl.when(row != 0)
    def _():
        remote(rp.at[own, :, 0:HALF], rp.at[own, :, 0:HALF], p1_s.at[0], p1_r, plane(0)).wait_recv()

    core_sends = [0]

    def core_panel(piece_rows, slot):
        src = rp.at[slot, piece_rows, 0:HALF]
        dst = po.at[slot, piece_rows]
        i = core_sends[0]
        core_sends[0] += 1
        send(src, dst, cp_s.at[i], cp_r.at[i], plane(core_row))

    whole = pl.ds(0, EB)
    send(rp.at[own], rp.at[own], br_s, br_r, to_ep)
    for direction in range(2):
        ring_send(rp, rs, rq, direction, 0, 0)
    core_panel(whole, own)
    other = (1 - ep) * 8 + col + 1
    remote(rp.at[other], rp.at[other], br_s, br_r, to_ep).wait_recv()
    for direction in range(2):
        ring_send(rp, rs, rq, direction, 0, 1)
    core_panel(whole, other)
    send(xr.at[own], xr.at[own], bx_s, bx_r, to_ep)
    for s in range(4):
        for k in range(2):
            for direction in range(2):
                ring_wait(rp, rs, rq, direction, s, k)
                if s < 3:
                    ring_send(rp, rs, rq, direction, s + 1, k)
                slot = eps[k] * 8 + ring_origin(direction, s + 1) + 1
                core_panel(whole if s < 3 else pl.ds(32 * direction, 32), slot)
    remote(xr.at[other], xr.at[other], bx_s, bx_r, to_ep).wait_recv()
    for direction in range(2):
        ring_send(xr, xs, xq, direction, 0, 1)

    q_own = row // 2
    mine8 = lambda k: pl.ds(k * 8 + 1, 8)

    def plane_send(i, q, dev_row, lo=0, n=8):
        piece = xc.at[q, pl.ds(core * 8 + 1 + lo, n)]
        send(piece, piece, c2_s.at[i], c2_r.at[i], plane(dev_row))

    def plane_wait(i, q, lo=0, n=8):
        piece = xc.at[q, pl.ds(core * 8 + 1 + lo, n)]
        remote(piece, piece, c2_s.at[i], c2_r.at[i], plane(core_row)).wait_recv()

    def core_send(i, q, lo=0, n=8):
        piece = xc.at[q, pl.ds(core * 8 + 1 + lo, n)]
        send(piece, piece, cc_s.at[i], cc_r.at[i], plane(core_row))

    def q_of(r):
        return r // 2

    q_x, q_up, q_down = q_of(x_row), q_of(yup_row), q_of(ydown_row)
    q_xup, q_xdown = q_of((x_row + 4) % 16), q_of((x_row + 12) % 16)
    q_opp, q_xopp = q_of((row + 8) % 16), q_of((x_row + 8) % 16)
    for z in range(8):
        piece = xc.at[q_own, core * 8 + z + 1]
        remote(piece, piece, c1_s.at[0], c1_r.at[z], plane(core_row)).wait_recv()
    plane_send(0, q_own, x_row)
    plane_send(1, q_own, yup_row)
    plane_send(2, q_own, ydown_row)
    core_send(0, q_own)

    arrivals = [(whole, own), (whole, other)]
    for s in range(4):
        for k in range(2):
            for direction in range(2):
                slot = eps[k] * 8 + ring_origin(direction, s + 1) + 1
                arrivals.append((whole if s < 3 else pl.ds(32 * direction, 32), slot))
    for i, (rows, slot) in enumerate(arrivals):
        remote(rp.at[slot, rows, 0:HALF], po.at[slot, rows], cp_s.at[i], cp_r.at[i], plane(core_row)).wait_recv()

    here = pl.ds(pl.multiple_of(core * HALF, HALF), HALF)
    there = pl.ds(pl.multiple_of((1 - core) * HALF, HALF), HALF)
    for e in range(NE):
        toep = rp[e + 1, :, HALF:]
        rows = slice(e * EB, (e + 1) * EB)
        pf[rows, here] = dot_nn(toep, rp[e : e + 2, :, :HALF].reshape(2 * EB, HALF)).astype(BF16)
        pf[rows, there] = dot_nn(toep, po[e : e + 2].reshape(2 * EB, HALF)).astype(BF16)
    for b in range(8):
        cut = slice(b * 128, (b + 1) * 128)
        pft[:, cut] = pf[cut, :].T
    smat[...] = dot_nn(pft[...], pf[...])
    di = lax.broadcasted_iota(jnp.int32, (PAN, PAN), 0)
    dj = lax.broadcasted_iota(jnp.int32, (PAN, PAN), 1)
    reg_diag = jnp.where(di == dj, reg_ref[:, :PAN], 0.0)
    smat[...] = smat[...] + reg_diag
    wmat[...] = jnp.zeros((PAN, PAN), F32)

    factor_step(smat, wmat, 0)

    def block_stage(s):
        for k in range(2):
            for direction in range(2):
                ring_wait(xr, xs, xq, direction, s, k)
                if s < 3:
                    ring_send(xr, xs, xq, direction, s + 1, k)

    block_stage(0)
    plane_wait(0, q_x)
    plane_send(3, q_x, yup_row)
    plane_send(4, q_x, ydown_row)
    core_send(1, q_x)
    plane_wait(1, q_down)
    plane_send(5, q_down, yup_row, 0, 4)
    core_send(2, q_down)
    plane_wait(2, q_up)
    plane_send(6, q_up, ydown_row, 4, 4)
    core_send(3, q_up)

    factor_step(smat, wmat, 1)
    block_stage(1)
    plane_wait(3, q_xdown)
    plane_send(7, q_xdown, yup_row, 0, 4)
    core_send(4, q_xdown)
    plane_wait(4, q_xup)
    plane_send(8, q_xup, ydown_row, 4, 4)
    core_send(5, q_xup)

    factor_step(smat, wmat, 2)
    block_stage(2)
    plane_wait(5, q_opp, 0, 4)
    plane_wait(6, q_opp, 4, 4)
    core_send(6, q_opp)
    plane_wait(7, q_xopp, 0, 4)
    plane_wait(8, q_xopp, 4, 4)
    core_send(7, q_xopp)

    factor_step(smat, wmat, 3)
    block_stage(3)
    for i, q in enumerate((q_own, q_x, q_down, q_up, q_xdown, q_xup, q_opp, q_xopp)):
        piece = xc.at[q, pl.ds((1 - core) * 8 + 1, 8)]
        remote(piece, piece, cc_s.at[i], cc_r.at[i], plane(core_row)).wait_recv()

    for e in range(0, NE, 2):
        pair = []
        for f in (e, e + 1):
            toep = rp[f + 1, :, HALF:]
            pair.append(dot_nn(toep, xr[f : f + 2].reshape(2 * EB, 1024)).astype(BF16))
            for q in range(8):
                fc_ref[f * EB : (f + 1) * EB, q * PB : (q + 1) * PB] = dot_nn(
                    toep, xc[q, f : f + 2].reshape(2 * EB, PB)
                ).astype(BF16)
        frt_ref[:, e * EB : (e + 2) * EB] = jnp.concatenate(pair, axis=0).T

    wh, wl = split2(wmat[...])
    wcat = jnp.concatenate([wh, wl, wh], axis=1)
    for b in range(2):
        cut = slice(b * PAN, (b + 1) * PAN)
        ar = dot_nn(frt_ref[cut, :], pf[...])
        if b == 0:
            ar = ar + jnp.where(row == 0, reg_diag, 0.0)
        ah, al = split2(ar)
        rr_ref[cut, :] = dot_nt(jnp.concatenate([ah, ah, al], axis=1), wcat)
        act = dot_nn(pft[...], fc_ref[:, cut])
        if b == 0:
            act = act + jnp.where(group == 0, reg_diag, 0.0)
        ah, al = split2(act)
        rct_ref[:, cut] = dot_nn(wcat, jnp.concatenate([ah, ah, al], axis=0))

    for copy in sends:
        copy.wait_send()
    for q in range(8):
        mine = jnp.logical_and(is_self, row // 2 == q)

        @pl.when(jnp.logical_not(mine))
        def _():
            remote(
                xr.at[own, :, q * PB : (q + 1) * PB], xc.at[q, own], c1_s.at[q], c1_r.at[col],
                {"ep": row // 8, "row": 2 * q + ep, "col": row % 8},
            ).wait_send()

    @pl.when(row == 0)
    def _():
        for t in range(1, 16):
            half = t % 2
            remote(
                xr.at[own, :, half * HALF : (half + 1) * HALF], rp.at[own, :, 0:HALF],
                p1_s.at[t - 1], p1_r, plane(t),
            ).wait_send()


def tile_kernel(frt_ref, fc_ref, rr_ref, rct_ref, reg_ref, out_ref, rcat):
    step = pl.program_id(0)
    rows_step = out_ref.shape[0]
    cols = out_ref.shape[1]
    row = lax.axis_index("row")
    group = lax.axis_index("ep") * 8 + lax.axis_index("col")

    @pl.when(step == 0)
    def _():
        rh, rl = split2(rct_ref[...])
        rcat[0:PAN] = rh
        rcat[PAN : 2 * PAN] = rl
        rcat[2 * PAN :] = rh

    base = row * 1024 + step * rows_step
    rr = rr_ref[...]
    ah, al = split2(rr)
    schur = dot_nn(jnp.concatenate([ah, ah, al], axis=1), rcat[...])
    tile = dot_nn(frt_ref[...], fc_ref[...])
    gr = base + lax.broadcasted_iota(jnp.int32, (rows_step, cols), 0)
    gc = group * 1024 + lax.broadcasted_iota(jnp.int32, (rows_step, cols), 1)
    reg = reg_ref[:, pl.ds(pl.multiple_of(group * 1024, 1024), 1024)]
    value = tile + jnp.where(gr == gc, reg, 0.0) - schur
    out_ref[...] = jnp.where(gr >= PAN, value, 0.0)

    @pl.when(group == 0)
    def _():
        pr = base + lax.broadcasted_iota(jnp.int32, (rows_step, PAN), 0)
        pc = lax.broadcasted_iota(jnp.int32, (rows_step, PAN), 1)
        out_ref[:, :PAN] = jnp.where(jnp.logical_and(pr < HALF, pc >= HALF), 0.0, rr)


def on_device(design, taps, tap_count, order, regular):
    vm = pl.BlockSpec(memory_space=pltpu.VMEM)
    dma = pltpu.SemaphoreType.DMA
    reg = regular.reshape(1, -1)
    frt, fc, rr, rct = pl.pallas_call(
        gather_kernel,
        out_shape=(
            jax.ShapeDtypeStruct((1024, 1024), BF16),
            jax.ShapeDtypeStruct((1024, 1024), BF16),
            jax.ShapeDtypeStruct((1024, PAN), F32),
            jax.ShapeDtypeStruct((PAN, 1024), F32),
        ),
        in_specs=[vm, pl.BlockSpec(memory_space=pltpu.SMEM), vm, vm, vm],
        out_specs=(vm, vm, vm, vm),
        scratch_shapes=[
            pltpu.VMEM((NE + 1, EB, 1024), BF16),
            pltpu.VMEM((8, NE + 1, EB, PB), BF16),
            pltpu.VMEM((NE + 1, EB, HALF + 128), BF16),
            pltpu.VMEM((NE + 1, EB, HALF), BF16),
            pltpu.VMEM((1024, PAN), BF16),
            pltpu.VMEM((PAN, 1024), BF16),
            pltpu.VMEM((PAN, PAN), F32),
            pltpu.VMEM((PAN, PAN), F32),
            dma, dma, dma, dma,
            dma((15,)), dma,
            dma((8,)), dma((8,)),
            dma((2, 4, 2)), dma((2, 4, 2)),
            dma((2, 4, 2)), dma((2, 4, 2)),
            dma((9,)), dma((9,)),
            dma((8,)), dma((8,)),
            dma((18,)), dma((18,)),
        ],
        compiler_params=pltpu.CompilerParams(
            collective_id=0, has_side_effects=True, vmem_limit_bytes=56 << 20
        ),
        name="gather",
    )(design, taps, tap_count.reshape(1, -1), order.reshape(1, -1), reg)
    rows_step = 128
    const = lambda shape: pl.BlockSpec(shape, lambda i: (0, 0), pipeline_mode=pl.Buffered(1))
    return pl.pallas_call(
        tile_kernel,
        grid=(1024 // rows_step,),
        out_shape=jax.ShapeDtypeStruct((1024, 1024), F32),
        in_specs=[
            pl.BlockSpec((rows_step, 1024), lambda i: (i, 0)),
            const((1024, 1024)),
            pl.BlockSpec((rows_step, PAN), lambda i: (i, 0)),
            const((PAN, 1024)),
            const((1, 16384)),
        ],
        out_specs=pl.BlockSpec((rows_step, 1024), lambda i: (i, 0)),
        scratch_shapes=[pltpu.VMEM((3 * PAN, 1024), BF16)],
        compiler_params=pltpu.CompilerParams(vmem_limit_bytes=40 << 20),
        name="tile",
    )(frt, fc, rr, rct, reg)


def solution(mesh):
    in_specs = (P(("ep", "col"), "row"), P(), P(("ep", "col")), P("row"), P())
    out_specs = P("row", ("ep", "col"))
    return jax.shard_map(
        on_device, mesh=mesh, in_specs=in_specs, out_specs=out_specs, check_vma=False
    )
```

```python
import functools

import jax
import jax.numpy as jnp
from jax import lax
from jax.experimental import pallas as pl
from jax.experimental.pallas import tpu as pltpu
from jax.sharding import PartitionSpec as P

MESH = pl.DeviceIdType.MESH
F32 = jnp.float32
BF16 = jnp.bfloat16
HIGHEST = lax.Precision.HIGHEST
PB = 128
PAN = 512
EB = 64
NE = 16
HALF = 256
QR = EB + 16


def dot_nn(a, b, precision=None):
    return lax.dot_general(
        a, b, (((1,), (0,)), ((), ())), precision=precision, preferred_element_type=F32
    )


def dot_nt(a, b, precision=None):
    return lax.dot_general(
        a, b, (((1,), (1,)), ((), ())), precision=precision, preferred_element_type=F32
    )


def split2(x):
    high = x.astype(BF16)
    return high, (x - high.astype(F32)).astype(BF16)


def lane_bcast(v, j):
    return jnp.broadcast_to(v[:, j : j + 1], (8, 128))


def row_bcast(v, k):
    return jnp.broadcast_to(v[k : k + 1, :], (8, 128))


def invert_factor(groups, hooks):
    sub = lax.broadcasted_iota(jnp.int32, (8, 128), 0)
    lane = lax.broadcasted_iota(jnp.int32, (8, 128), 1)
    a = list(groups)
    g = [jnp.where(lane == sub + 8 * q, 1.0, 0.0).astype(F32) for q in range(16)]
    for p in range(16):
        v = a[p]
        c = [lane_bcast(v, 8 * p + k) for k in range(8)]
        s = [[None] * 8 for _ in range(8)]
        for k in range(8):
            for i in range(k, 8):
                s[i][k] = row_bcast(c[k], i)
        rinv = [None] * 8
        lcol = [None] * 8
        dvec = None
        gp = g[p]
        for k in range(8):
            r = 1.0 / s[k][k]
            rinv[k] = r
            for i in range(k + 1, 8):
                m = s[i][k] * r
                for j in range(k + 1, i + 1):
                    s[i][j] = s[i][j] - m * s[j][k]
            if k < 7:
                lcol[k] = jnp.where(sub > k, c[k] * r, 0.0)
                for m in range(k + 1, 8):
                    c[m] = c[m] - lcol[k] * s[m][k]
            dvec = s[k][k] if dvec is None else jnp.where(sub == k, s[k][k], dvec)
        vrow = [None] * 8
        grow = [None] * 8
        for k in range(8):
            vrow[k] = row_bcast(v, k)
            grow[k] = row_bcast(gp, k)
            if k < 7:
                v = v - lcol[k] * vrow[k]
                gp = gp - lcol[k] * grow[k]
        for q in range(p + 1, 16):
            d = [lane_bcast(a[q], 8 * p + k) for k in range(8)]
            for k in range(8):
                d[k] = d[k] * rinv[k]
                for m in range(k + 1, 8):
                    d[m] = d[m] - d[k] * s[m][k]
            aq, gq = a[q], g[q]
            for k in range(8):
                aq = aq - d[k] * vrow[k]
                gq = gq - d[k] * grow[k]
            a[q], g[q] = aq, gq
        g[p] = gp * lax.rsqrt(dvec)
        if p in hooks:
            hooks[p]()
    return g


def factor_step(s, w, b, hooks={}):
    n = s.shape[0]
    lo, hi = 128 * b, 128 * b + 128
    g = invert_factor([s[lo + 8 * q : lo + 8 * q + 8, lo:hi] for q in range(16)], hooks)
    for q in range(16):
        w[lo + 8 * q : lo + 8 * q + 8, lo:hi] = g[q]
    inv = w[lo:hi, lo:hi]
    if b > 0:
        w[lo:hi, :lo] = dot_nn(inv, w[lo:hi, :lo], HIGHEST)
    if hi < n:
        below = dot_nt(s[hi:, lo:hi], inv, HIGHEST)
        s[hi:, hi:] = s[hi:, hi:] - dot_nt(below, below, HIGHEST)
        w[hi:, :hi] = w[hi:, :hi] - dot_nn(below, w[lo:hi, :hi], HIGHEST)


def gather_kernel(
    design_in, taps_in, count_in, order_in, reg_in,
    frt_ref, fc_ref, rr_ref, rct_ref, regc_ref,
    xr, xc, pq, band_ref, pf, pft, smat, wmat,
    design_ref, taps_ref, count_ref, order_ref, reg_ref,
    in_s, bx_s, bx_r, p1_s, p1_r, c1_s, c1_r, xs, xq, gr_s, gr_r, px_s, px_r, po_s, po_r, pc_s, pc_r,
    c2_s, c2_r, cc_s, cc_r,
):
    group = lax.axis_index("ep") * 8 + lax.axis_index("col")
    loads = [
        pltpu.make_async_copy(order_in, order_ref, in_s.at[0]),
        pltpu.make_async_copy(design_in, design_ref, in_s.at[1]),
        pltpu.make_async_copy(taps_in, taps_ref, in_s.at[2]),
        pltpu.make_async_copy(count_in, count_ref, in_s.at[3]),
        pltpu.make_async_copy(reg_in.at[:, pl.ds(0, PAN)], reg_ref, in_s.at[4]),
        pltpu.make_async_copy(
            reg_in.at[:, pl.ds(pl.multiple_of(group * 1024, 1024), 1024)], regc_ref, in_s.at[5]
        ),
    ]
    for load in loads:
        load.start()
    ep = lax.axis_index("ep")
    row = lax.axis_index("row")
    col = lax.axis_index("col")
    core = row % 2
    e_own = ep * 8 + col
    line = row % 4
    up, down = (col + 1) % 8, (col + 7) % 8
    to_up = {"ep": ep, "row": row, "col": up}
    to_down = {"ep": ep, "row": row, "col": down}
    to_ep = {"ep": 1 - ep, "row": row, "col": col}
    core_row = row - core + (1 - core)
    xlo = (row // 2) % 2
    x_row = row + 2 - 4 * xlo
    yup_row, ydown_row = (row + 4) % 16, (row + 12) % 16
    plane = lambda r: {"ep": ep, "row": r, "col": col}
    is_self = jnp.logical_and(row == group, core == ep)

    barrier = pltpu.get_barrier_semaphore()
    for dev in (plane(core_row), plane(x_row), plane(yup_row), plane(ydown_row)):
        pl.semaphore_signal(barrier, inc=1, device_id=dev, device_id_type=MESH)
    mates = []
    for dz, de in ((1, 0), (7, 0), (0, 1), (2, 0), (6, 0), (1, 1), (7, 1), (3, 0), (5, 0), (2, 1), (6, 1), (4, 0), (3, 1), (5, 1), (4, 1)):
        mate_ep, mate_col = (ep + de) % 2, (col + dz) % 8
        mates.append((mate_ep, mate_col))
        pl.semaphore_signal(
            barrier, inc=1, device_id={"ep": mate_ep, "row": row, "col": mate_col}, device_id_type=MESH
        )

    @pl.when(row != 0)
    def _():
        pl.semaphore_signal(barrier, inc=1, device_id=plane(0), device_id_type=MESH)

    for z in range(8):
        mine = jnp.logical_and(is_self, col == z)

        @pl.when(jnp.logical_not(mine))
        def _():
            pl.semaphore_signal(
                barrier, inc=1, device_id={"ep": core, "row": group, "col": z}, device_id_type=MESH
            )

    for load in loads:
        load.wait()
    local = order_ref[...] % PB
    kk = lax.broadcasted_iota(jnp.int32, (PB, 1024), 0)
    one_hot = jnp.where(kk == local, 1.0, 0.0).astype(BF16)
    own = e_own + 1
    for g in range(8):
        part = dot_nn(design_ref[:, g * PB : (g + 1) * PB], one_hot[:, g * PB : (g + 1) * PB])
        xr[own, :, g * PB : (g + 1) * PB] = part.astype(BF16)
    ii = lax.broadcasted_iota(jnp.int32, (EB, 128), 0)
    jj = lax.broadcasted_iota(jnp.int32, (EB, 128), 1)
    lag = ii + EB - jj
    ti = lax.broadcasted_iota(jnp.int32, (EB, EB), 0)
    tj = lax.broadcasted_iota(jnp.int32, (EB, EB), 1)
    counts = jnp.sum(jnp.where(ti == tj, count_ref[...].astype(F32), 0.0), axis=1, keepdims=True)
    band = jnp.zeros((EB, 128), F32)
    for t in range(taps_ref.shape[0]):
        band = jnp.where(lag == t, taps_ref[t], band)
    band = jnp.where(lag.astype(F32) < counts, band, 0.0)
    band_ref[...] = band.astype(BF16)
    pq[line, own, EB:, :] = band_ref[pl.ds(pl.multiple_of(16 * line, 16), 16), :]
    xr[0] = jnp.zeros(xr.shape[1:], BF16)
    for u in range(4):
        pq[u, 0] = jnp.zeros((QR, 128), BF16)
    for q in range(8):
        xc[q, 0] = jnp.zeros((EB, PB), BF16)

    @pl.when(row == 0)
    def _():
        pq[0, own, :EB, :] = xr[own, :, :128]

    pl.semaphore_wait(
        barrier, 4 + 15 + 8 + jnp.where(row == 0, 15, 0) - jnp.where(is_self, 1, 0)
    )

    sends = []

    def remote(src, dst, s_sem, r_sem, dev):
        return pltpu.make_async_remote_copy(
            src_ref=src, dst_ref=dst, send_sem=s_sem, recv_sem=r_sem, device_id=dev, device_id_type=MESH
        )

    def send(src, dst, s_sem, r_sem, dev):
        copy = remote(src, dst, s_sem, r_sem, dev)
        copy.start()
        sends.append(copy)

    @pl.when(row == 0)
    def _():
        for t in range(1, 16):
            u = t % 4
            remote(
                xr.at[own, :, u * 128 : (u + 1) * 128], pq.at[u, own, 0:EB],
                p1_s.at[t - 1], p1_r, plane(t),
            ).start()

    eps = (ep, 1 - ep)

    def ring_origin(direction, s):
        return (col + 8 - s) % 8 if direction == 0 else (col + s) % 8

    def ring_piece(buf, k, z, direction, s):
        slot = eps[k] * 8 + z + 1
        if s < 3:
            return buf.at[slot]
        return buf.at[slot, pl.ds(32 * direction, 32)]

    def ring_send(buf, ssem, rsem, direction, s, k):
        piece = ring_piece(buf, k, ring_origin(direction, s), direction, s)
        send(piece, piece, ssem.at[direction, s, k], rsem.at[direction, s, k], (to_up, to_down)[direction])

    def ring_wait(buf, ssem, rsem, direction, s, k):
        piece = ring_piece(buf, k, ring_origin(direction, s + 1), direction, s)
        remote(piece, piece, ssem.at[direction, s, k], rsem.at[direction, s, k], to_up).wait_recv()

    for direction in range(2):
        ring_send(xr, xs, xq, direction, 0, 0)
    for q in range(8):
        src = xr.at[own, :, q * PB : (q + 1) * PB]
        dst = xc.at[q, own]
        mine = jnp.logical_and(is_self, row // 2 == q)

        @pl.when(jnp.logical_not(mine))
        def _():
            remote(
                src, dst, c1_s.at[q], c1_r.at[col],
                {"ep": row // 8, "row": 2 * q + ep, "col": row % 8},
            ).start()

        @pl.when(mine)
        def _():
            pltpu.make_async_copy(src, dst, c1_r.at[col]).start()

    send(xr.at[own], xr.at[own], bx_s, bx_r, to_ep)

    @pl.when(row != 0)
    def _():
        piece = pq.at[line, own, 0:EB]
        remote(piece, piece, p1_s.at[0], p1_r, plane(0)).wait_recv()

    x_line = (line + 2) % 4
    back = (1, 0, 2, 4, 3, 6, 5, 8, 7, 10, 9, 11, 13, 12, 14)
    slots = [own] + [a * 8 + z + 1 for a, z in mates]

    def quarter_spread(i):
        piece = pq.at[line, slots[i]]
        send(piece, piece, px_s.at[i], px_r.at[i], plane(x_row))
        send(piece, piece, po_s.at[i], po_r.at[i], plane(core_row))

    def quarter_wait(i):
        piece = pq.at[line, slots[i + 1]]
        remote(piece, piece, gr_s.at[i], gr_r.at[back[i]], to_up).wait_recv()

    def block_stage(s, k):
        for direction in range(2):
            ring_wait(xr, xs, xq, direction, s, k)
            if s < 3:
                ring_send(xr, xs, xq, direction, s + 1, k)

    q_own = row // 2

    def plane_send(i, q, dev_row, lo=0, n=8):
        piece = xc.at[q, pl.ds(core * 8 + 1 + lo, n)]
        send(piece, piece, c2_s.at[i], c2_r.at[i], plane(dev_row))

    def plane_wait(i, q, lo=0, n=8):
        piece = xc.at[q, pl.ds(core * 8 + 1 + lo, n)]
        remote(piece, piece, c2_s.at[i], c2_r.at[i], plane(core_row)).wait_recv()

    def core_send(i, q):
        piece = xc.at[q, pl.ds(core * 8 + 1, 8)]
        send(piece, piece, cc_s.at[i], cc_r.at[i], plane(core_row))

    q_x, q_up, q_down = x_row // 2, yup_row // 2, ydown_row // 2
    q_xup, q_xdown = ((x_row + 4) % 16) // 2, ((x_row + 12) % 16) // 2
    q_opp, q_xopp = ((row + 8) % 16) // 2, ((x_row + 8) % 16) // 2

    own_quarter = pq.at[line, own]
    for i, (a, z) in enumerate(mates):
        send(own_quarter, own_quarter, gr_s.at[i], gr_r.at[i], {"ep": a, "row": row, "col": z})
    quarter_spread(0)
    for i in range(15):
        quarter_wait(i)
        quarter_spread(i + 1)
    for i in range(16):
        piece = pq.at[x_line, slots[i]]
        remote(piece, piece, px_s.at[i], px_r.at[i], plane(x_row)).wait_recv()
        send(piece, piece, pc_s.at[i], pc_r.at[i], plane(core_row))
    other = (1 - ep) * 8 + col + 1
    remote(xr.at[other], xr.at[other], bx_s, bx_r, to_ep).wait_recv()
    for direction in range(2):
        ring_send(xr, xs, xq, direction, 0, 1)
    block_stage(0, 0)
    for z in range(8):
        piece = xc.at[q_own, core * 8 + z + 1]
        remote(piece, piece, c1_s.at[0], c1_r.at[z], plane(core_row)).wait_recv()
    plane_send(0, q_own, x_row)
    plane_send(1, q_own, yup_row)
    plane_send(2, q_own, ydown_row)
    core_send(0, q_own)
    core_line = line + 1 - 2 * core
    for i in range(16):
        piece = pq.at[core_line, slots[i]]
        remote(piece, piece, po_s.at[i], po_r.at[i], plane(core_row)).wait_recv()
    core_line = (core_line + 2) % 4
    for i in range(16):
        piece = pq.at[core_line, slots[i]]
        remote(piece, piece, pc_s.at[i], pc_r.at[i], plane(core_row)).wait_recv()

    for e in range(NE):
        toep = jnp.concatenate([pq[u, e + 1, EB:, :] for u in range(4)], axis=0)
        panel = jnp.concatenate(
            [jnp.concatenate([pq[u, e, :EB, :], pq[u, e + 1, :EB, :]], axis=0) for u in range(4)], axis=1
        )
        pf[e * EB : (e + 1) * EB, :] = dot_nn(toep, panel).astype(BF16)
    for b in range(8):
        cut = slice(b * 128, (b + 1) * 128)
        pft[:, cut] = pf[cut, :].T
    smat[...] = dot_nn(pft[...], pf[...])
    di = lax.broadcasted_iota(jnp.int32, (PAN, PAN), 0)
    dj = lax.broadcasted_iota(jnp.int32, (PAN, PAN), 1)
    reg_diag = jnp.where(di == dj, reg_ref[...], 0.0)
    smat[...] = smat[...] + reg_diag
    wmat[...] = jnp.zeros((PAN, PAN), F32)

    def stage_a():
        block_stage(0, 1)
        plane_wait(0, q_x)
        plane_send(3, q_x, yup_row)
        plane_send(4, q_x, ydown_row)
        core_send(1, q_x)
        plane_wait(1, q_down)
        plane_send(5, q_down, yup_row, 0, 4)
        plane_wait(2, q_up)
        plane_send(6, q_up, ydown_row, 4, 4)

    def stage_b():
        block_stage(1, 0)
        core_send(2, q_down)
        core_send(3, q_up)

    def stage_c():
        plane_wait(3, q_xdown)
        plane_send(7, q_xdown, yup_row, 0, 4)
        core_send(4, q_xdown)
        plane_wait(4, q_xup)
        plane_send(8, q_xup, ydown_row, 4, 4)
        core_send(5, q_xup)

    def stage_d():
        block_stage(1, 1)

    def stage_e():
        block_stage(2, 0)

    def stage_f():
        block_stage(2, 1)
        plane_wait(5, q_opp, 0, 4)
        plane_wait(6, q_opp, 4, 4)
        core_send(6, q_opp)
        plane_wait(7, q_xopp, 0, 4)
        plane_wait(8, q_xopp, 4, 4)
        core_send(7, q_xopp)

    factor_step(smat, wmat, 0, {11: stage_a})
    factor_step(smat, wmat, 1, {3: stage_b, 11: stage_c, 15: stage_d})
    factor_step(smat, wmat, 2, {7: stage_e, 15: stage_f})
    factor_step(smat, wmat, 3)
    block_stage(3, 0)
    block_stage(3, 1)
    for i, q in enumerate((q_own, q_x, q_down, q_up, q_xdown, q_xup, q_opp, q_xopp)):
        piece = xc.at[q, pl.ds((1 - core) * 8 + 1, 8)]
        remote(piece, piece, cc_s.at[i], cc_r.at[i], plane(core_row)).wait_recv()

    for e in range(0, NE, 2):
        pair = []
        for f in (e, e + 1):
            toep = jnp.concatenate([pq[u, f + 1, EB:, :] for u in range(4)], axis=0)
            pair.append(dot_nn(toep, xr[f : f + 2].reshape(2 * EB, 1024)).astype(BF16))
            for q in range(8):
                fc_ref[f * EB : (f + 1) * EB, q * PB : (q + 1) * PB] = dot_nn(
                    toep, xc[q, f : f + 2].reshape(2 * EB, PB)
                ).astype(BF16)
        frt_ref[:, e * EB : (e + 2) * EB] = jnp.concatenate(pair, axis=0).T

    wh, wl = split2(wmat[...])
    wcat = jnp.concatenate([wh, wl, wh], axis=1)
    for b in range(2):
        cut = slice(b * PAN, (b + 1) * PAN)
        ar = dot_nn(frt_ref[cut, :], pf[...])
        if b == 0:
            ar = ar + jnp.where(row == 0, reg_diag, 0.0)
        ah, al = split2(ar)
        rr_ref[cut, :] = dot_nt(jnp.concatenate([ah, ah, al], axis=1), wcat)
        act = dot_nn(pft[...], fc_ref[:, cut])
        if b == 0:
            act = act + jnp.where(group == 0, reg_diag, 0.0)
        ah, al = split2(act)
        rct_ref[:, cut] = dot_nn(wcat, jnp.concatenate([ah, ah, al], axis=0))

    for copy in sends:
        copy.wait_send()
    for q in range(8):
        mine = jnp.logical_and(is_self, row // 2 == q)

        @pl.when(jnp.logical_not(mine))
        def _():
            remote(
                xr.at[own, :, q * PB : (q + 1) * PB], xc.at[q, own], c1_s.at[q], c1_r.at[col],
                {"ep": row // 8, "row": 2 * q + ep, "col": row % 8},
            ).wait_send()

    @pl.when(row == 0)
    def _():
        for t in range(1, 16):
            u = t % 4
            remote(
                xr.at[own, :, u * 128 : (u + 1) * 128], pq.at[u, own, 0:EB],
                p1_s.at[t - 1], p1_r, plane(t),
            ).wait_send()


def tile_kernel(frt_ref, fc_ref, rr_ref, rct_ref, reg_ref, out_ref, rcat):
    step = pl.program_id(0)
    rows_step = out_ref.shape[0]
    cols = out_ref.shape[1]
    row = lax.axis_index("row")
    group = lax.axis_index("ep") * 8 + lax.axis_index("col")

    @pl.when(step == 0)
    def _():
        rh, rl = split2(rct_ref[...])
        rcat[0:PAN] = rh
        rcat[PAN : 2 * PAN] = rl
        rcat[2 * PAN :] = rh

    base = row * 1024 + step * rows_step
    here = pl.ds(pl.multiple_of(step * rows_step, rows_step), rows_step)
    rr = rr_ref[here, :]
    ah, al = split2(rr)
    schur = dot_nn(jnp.concatenate([ah, ah, al], axis=1), rcat[...])
    tile = dot_nn(frt_ref[here, :], fc_ref[...])
    gr = base + lax.broadcasted_iota(jnp.int32, (rows_step, cols), 0)
    gc = group * 1024 + lax.broadcasted_iota(jnp.int32, (rows_step, cols), 1)
    reg = reg_ref[...]
    value = tile + jnp.where(gr == gc, reg, 0.0) - schur
    out_ref[...] = jnp.where(gr >= PAN, value, 0.0)

    @pl.when(group == 0)
    def _():
        pr = base + lax.broadcasted_iota(jnp.int32, (rows_step, PAN), 0)
        pc = lax.broadcasted_iota(jnp.int32, (rows_step, PAN), 1)
        out_ref[:, :PAN] = jnp.where(jnp.logical_and(pr < HALF, pc >= HALF), 0.0, rr)


def on_device(design, taps, tap_count, order, regular):
    vm = pl.BlockSpec(memory_space=pltpu.VMEM)
    dma = pltpu.SemaphoreType.DMA
    reg = regular.reshape(1, -1)
    frt, fc, rr, rct, regc = pl.pallas_call(
        gather_kernel,
        out_shape=(
            pltpu.VMEM((1024, 1024), BF16),
            pltpu.VMEM((1024, 1024), BF16),
            pltpu.VMEM((1024, PAN), F32),
            pltpu.VMEM((PAN, 1024), F32),
            pltpu.VMEM((1, 1024), F32),
        ),
        in_specs=[pl.BlockSpec(memory_space=pltpu.HBM)] * 5,
        out_specs=(vm, vm, vm, vm, vm),
        scratch_shapes=[
            pltpu.VMEM((NE + 1, EB, 1024), BF16),
            pltpu.VMEM((8, NE + 1, EB, PB), BF16),
            pltpu.VMEM((4, NE + 1, QR, 128), BF16),
            pltpu.VMEM((EB, 128), BF16),
            pltpu.VMEM((1024, PAN), BF16),
            pltpu.VMEM((PAN, 1024), BF16),
            pltpu.VMEM((PAN, PAN), F32),
            pltpu.VMEM((PAN, PAN), F32),
            pltpu.VMEM((EB, 1024), BF16),
            pltpu.SMEM((64,), F32),
            pltpu.VMEM((1, EB), jnp.int32),
            pltpu.VMEM((1, 1024), jnp.int32),
            pltpu.VMEM((1, PAN), F32),
            dma((6,)),
            dma, dma,
            dma((15,)), dma,
            dma((8,)), dma((8,)),
            dma((2, 4, 2)), dma((2, 4, 2)),
            dma((15,)), dma((15,)),
            dma((16,)), dma((16,)),
            dma((16,)), dma((16,)),
            dma((16,)), dma((16,)),
            dma((9,)), dma((9,)),
            dma((8,)), dma((8,)),
        ],
        compiler_params=pltpu.CompilerParams(
            collective_id=0, has_side_effects=True, vmem_limit_bytes=58450000
        ),
        name="gather",
    )(design, taps, tap_count.reshape(1, -1), order.reshape(1, -1), reg)
    rows_step = 128
    return pl.pallas_call(
        tile_kernel,
        grid=(1024 // rows_step,),
        out_shape=jax.ShapeDtypeStruct((1024, 1024), F32),
        in_specs=[
            vm, vm, vm, vm, vm,
        ],
        out_specs=pl.BlockSpec((rows_step, 1024), lambda i: (i, 0)),
        scratch_shapes=[pltpu.VMEM((3 * PAN, 1024), BF16)],
        compiler_params=pltpu.CompilerParams(vmem_limit_bytes=36 << 20),
        name="tile",
    )(frt, fc, rr, rct, regc)


def solution(mesh):
    in_specs = (P(("ep", "col"), "row"), P(), P(("ep", "col")), P("row"), P())
    out_specs = P("row", ("ep", "col"))
    return jax.shard_map(
        on_device, mesh=mesh, in_specs=in_specs, out_specs=out_specs, check_vma=False
    )
```

```python
import functools

import jax
import jax.numpy as jnp
from jax import lax
from jax.experimental import pallas as pl
from jax.experimental.pallas import tpu as pltpu
from jax.sharding import PartitionSpec as P

MESH = pl.DeviceIdType.MESH
F32 = jnp.float32
BF16 = jnp.bfloat16
HIGHEST = lax.Precision.HIGHEST
PB = 128
PAN = 512
EB = 64
NE = 16
HALF = 256
QR = EB + 16


def dot_nn(a, b, precision=None):
    return lax.dot_general(
        a, b, (((1,), (0,)), ((), ())), precision=precision, preferred_element_type=F32
    )


def dot_nt(a, b, precision=None):
    return lax.dot_general(
        a, b, (((1,), (1,)), ((), ())), precision=precision, preferred_element_type=F32
    )


def split2(x):
    high = x.astype(BF16)
    return high, (x - high.astype(F32)).astype(BF16)


def lane_bcast(v, j):
    return jnp.broadcast_to(v[:, j : j + 1], (8, 128))


def reciprocal(x):
    r = pl.reciprocal(x, approx=True)
    r = r * (2.0 - x * r)
    return r * (2.0 - x * r)


def invert_factor(groups, spread, hooks):
    sub = lax.broadcasted_iota(jnp.int32, (8, 128), 0)
    lane = lax.broadcasted_iota(jnp.int32, (8, 128), 1)
    a = list(groups)
    out = [None] * 16
    for p in range(16):
        base = (p % 2) * 72
        v = a[p]
        c = [lane_bcast(v, 8 * p + k) for k in range(8)]
        here = (lane >= 8 * p) & (lane < 8 * p + 8)
        m = jnp.where(here, jnp.where(lane - 8 * p == sub, 1.0, 0.0), v)
        for k in range(8):
            spread[base + 8 * k : base + 8 * k + 8, :] = c[k]
        spread[base + 64 : base + 72, :] = m
        s = [[None] * 8 for _ in range(8)]
        for k in range(8):
            for i in range(k, 8):
                s[i][k] = spread[pl.ds(base + 8 * k + i, 8, stride=0), :]
        rows = [spread[pl.ds(base + 64 + k, 8, stride=0), :] for k in range(8)]
        later = range(p + 1, 16)
        d = {q: [lane_bcast(a[q], 8 * p + k) for k in range(8)] for q in later}
        for q in later:
            a[q] = jnp.where(here, 0.0, a[q])
        for k in range(8):
            r = reciprocal(s[k][k])
            for i in range(k + 1, 8):
                w = s[i][k] * r
                for j in range(k + 1, i + 1):
                    s[i][j] = s[i][j] - w * s[j][k]
                rows[i] = rows[i] - w * rows[k]
            for q in later:
                w = d[q][k] * r
                for i in range(k + 1, 8):
                    d[q][i] = d[q][i] - w * s[i][k]
                a[q] = a[q] - w * rows[k]
        done = rows[0] * lax.rsqrt(s[0][0])
        for k in range(1, 8):
            done = jnp.where(sub == k, rows[k] * lax.rsqrt(s[k][k]), done)
        out[p] = jnp.where(lane < 8 * p + 8, done, 0.0)
        if p in hooks:
            hooks[p]()
    return out


def factor_step(s, w, spread, b, hooks={}):
    n = s.shape[0]
    lo, hi = 128 * b, 128 * b + 128
    g = invert_factor([s[lo + 8 * q : lo + 8 * q + 8, lo:hi] for q in range(16)], spread, hooks)
    for q in range(16):
        w[lo + 8 * q : lo + 8 * q + 8, lo:hi] = g[q]
    inv = w[lo:hi, lo:hi]
    if b > 0:
        w[lo:hi, :lo] = dot_nn(inv, w[lo:hi, :lo], HIGHEST)
    if hi < n:
        below = dot_nt(s[hi:, lo:hi], inv, HIGHEST)
        s[hi:, hi:] = s[hi:, hi:] - dot_nt(below, below, HIGHEST)
        w[hi:, :hi] = w[hi:, :hi] - dot_nn(below, w[lo:hi, :hi], HIGHEST)


def gather_kernel(
    design_in, taps_in, count_in, order_in, reg_in,
    frt_ref, fc_ref, rr_ref, rct_ref, regc_ref,
    xr, xc, pq, band_ref, pf, pft, smat, wmat, spread,
    design_ref, taps_ref, count_ref, order_ref, reg_ref,
    in_s, bx_s, bx_r, p1_s, p1_r, c1_s, c1_r, xs, xq, gr_s, gr_r, px_s, px_r, po_s, po_r, pc_s, pc_r,
    c2_s, c2_r, cc_s, cc_r,
):
    group = lax.axis_index("ep") * 8 + lax.axis_index("col")
    loads = [
        pltpu.make_async_copy(order_in, order_ref, in_s.at[0]),
        pltpu.make_async_copy(design_in, design_ref, in_s.at[1]),
        pltpu.make_async_copy(taps_in, taps_ref, in_s.at[2]),
        pltpu.make_async_copy(count_in, count_ref, in_s.at[3]),
        pltpu.make_async_copy(reg_in.at[:, pl.ds(0, PAN)], reg_ref, in_s.at[4]),
        pltpu.make_async_copy(
            reg_in.at[:, pl.ds(pl.multiple_of(group * 1024, 1024), 1024)], regc_ref, in_s.at[5]
        ),
    ]
    for load in loads:
        load.start()
    ep = lax.axis_index("ep")
    row = lax.axis_index("row")
    col = lax.axis_index("col")
    core = row % 2
    e_own = ep * 8 + col
    line = row % 4
    up, down = (col + 1) % 8, (col + 7) % 8
    to_up = {"ep": ep, "row": row, "col": up}
    to_down = {"ep": ep, "row": row, "col": down}
    to_ep = {"ep": 1 - ep, "row": row, "col": col}
    core_row = row - core + (1 - core)
    xlo = (row // 2) % 2
    x_row = row + 2 - 4 * xlo
    yup_row, ydown_row = (row + 4) % 16, (row + 12) % 16
    plane = lambda r: {"ep": ep, "row": r, "col": col}
    is_self = jnp.logical_and(row == group, core == ep)

    barrier = pltpu.get_barrier_semaphore()
    for dev in (plane(core_row), plane(x_row), plane(yup_row), plane(ydown_row)):
        pl.semaphore_signal(barrier, inc=1, device_id=dev, device_id_type=MESH)
    mates = []
    for dz, de in ((1, 0), (7, 0), (0, 1), (2, 0), (6, 0), (1, 1), (7, 1), (3, 0), (5, 0), (2, 1), (6, 1), (4, 0), (3, 1), (5, 1), (4, 1)):
        mate_ep, mate_col = (ep + de) % 2, (col + dz) % 8
        mates.append((mate_ep, mate_col))
        pl.semaphore_signal(
            barrier, inc=1, device_id={"ep": mate_ep, "row": row, "col": mate_col}, device_id_type=MESH
        )

    @pl.when(row != 0)
    def _():
        pl.semaphore_signal(barrier, inc=1, device_id=plane(0), device_id_type=MESH)

    for z in range(8):
        mine = jnp.logical_and(is_self, col == z)

        @pl.when(jnp.logical_not(mine))
        def _():
            pl.semaphore_signal(
                barrier, inc=1, device_id={"ep": core, "row": group, "col": z}, device_id_type=MESH
            )

    for load in loads:
        load.wait()
    local = order_ref[...] % PB
    kk = lax.broadcasted_iota(jnp.int32, (PB, 1024), 0)
    one_hot = jnp.where(kk == local, 1.0, 0.0).astype(BF16)
    own = e_own + 1
    for g in range(8):
        part = dot_nn(design_ref[:, g * PB : (g + 1) * PB], one_hot[:, g * PB : (g + 1) * PB])
        xr[own, :, g * PB : (g + 1) * PB] = part.astype(BF16)
    ii = lax.broadcasted_iota(jnp.int32, (EB, 128), 0)
    jj = lax.broadcasted_iota(jnp.int32, (EB, 128), 1)
    lag = ii + EB - jj
    ti = lax.broadcasted_iota(jnp.int32, (EB, EB), 0)
    tj = lax.broadcasted_iota(jnp.int32, (EB, EB), 1)
    counts = jnp.sum(jnp.where(ti == tj, count_ref[...].astype(F32), 0.0), axis=1, keepdims=True)
    band = jnp.zeros((EB, 128), F32)
    for t in range(taps_ref.shape[0]):
        band = jnp.where(lag == t, taps_ref[t], band)
    band = jnp.where(lag.astype(F32) < counts, band, 0.0)
    band_ref[...] = band.astype(BF16)
    pq[line, own, EB:, :] = band_ref[pl.ds(pl.multiple_of(16 * line, 16), 16), :]
    xr[0] = jnp.zeros(xr.shape[1:], BF16)
    for u in range(4):
        pq[u, 0] = jnp.zeros((QR, 128), BF16)
    for q in range(8):
        xc[q, 0] = jnp.zeros((EB, PB), BF16)

    @pl.when(row == 0)
    def _():
        pq[0, own, :EB, :] = xr[own, :, :128]

    pl.semaphore_wait(
        barrier, 4 + 15 + 8 + jnp.where(row == 0, 15, 0) - jnp.where(is_self, 1, 0)
    )

    sends = []

    def remote(src, dst, s_sem, r_sem, dev):
        return pltpu.make_async_remote_copy(
            src_ref=src, dst_ref=dst, send_sem=s_sem, recv_sem=r_sem, device_id=dev, device_id_type=MESH
        )

    def send(src, dst, s_sem, r_sem, dev):
        copy = remote(src, dst, s_sem, r_sem, dev)
        copy.start()
        sends.append(copy)

    @pl.when(row == 0)
    def _():
        for t in range(1, 16):
            u = t % 4
            remote(
                xr.at[own, :, u * 128 : (u + 1) * 128], pq.at[u, own, 0:EB],
                p1_s.at[t - 1], p1_r, plane(t),
            ).start()

    eps = (ep, 1 - ep)

    def ring_origin(direction, s):
        return (col + 8 - s) % 8 if direction == 0 else (col + s) % 8

    def ring_piece(buf, k, z, direction, s):
        slot = eps[k] * 8 + z + 1
        if s < 3:
            return buf.at[slot]
        return buf.at[slot, pl.ds(32 * direction, 32)]

    def ring_send(buf, ssem, rsem, direction, s, k):
        piece = ring_piece(buf, k, ring_origin(direction, s), direction, s)
        send(piece, piece, ssem.at[direction, s, k], rsem.at[direction, s, k], (to_up, to_down)[direction])

    def ring_wait(buf, ssem, rsem, direction, s, k):
        piece = ring_piece(buf, k, ring_origin(direction, s + 1), direction, s)
        remote(piece, piece, ssem.at[direction, s, k], rsem.at[direction, s, k], to_up).wait_recv()

    for direction in range(2):
        ring_send(xr, xs, xq, direction, 0, 0)
    for q in range(8):
        src = xr.at[own, :, q * PB : (q + 1) * PB]
        dst = xc.at[q, own]
        mine = jnp.logical_and(is_self, row // 2 == q)

        @pl.when(jnp.logical_not(mine))
        def _():
            remote(
                src, dst, c1_s.at[q], c1_r.at[col],
                {"ep": row // 8, "row": 2 * q + ep, "col": row % 8},
            ).start()

        @pl.when(mine)
        def _():
            pltpu.make_async_copy(src, dst, c1_r.at[col]).start()

    send(xr.at[own], xr.at[own], bx_s, bx_r, to_ep)

    @pl.when(row != 0)
    def _():
        piece = pq.at[line, own, 0:EB]
        remote(piece, piece, p1_s.at[0], p1_r, plane(0)).wait_recv()

    x_line = (line + 2) % 4
    back = (1, 0, 2, 4, 3, 6, 5, 8, 7, 10, 9, 11, 13, 12, 14)
    slots = [own] + [a * 8 + z + 1 for a, z in mates]

    def quarter_spread(i):
        piece = pq.at[line, slots[i]]
        send(piece, piece, px_s.at[i], px_r.at[i], plane(x_row))
        send(piece, piece, po_s.at[i], po_r.at[i], plane(core_row))

    def quarter_wait(i):
        piece = pq.at[line, slots[i + 1]]
        remote(piece, piece, gr_s.at[i], gr_r.at[back[i]], to_up).wait_recv()

    def block_stage(s, k):
        for direction in range(2):
            ring_wait(xr, xs, xq, direction, s, k)
            if s < 3:
                ring_send(xr, xs, xq, direction, s + 1, k)

    q_own = row // 2

    def plane_send(i, q, dev_row, lo=0, n=8):
        piece = xc.at[q, pl.ds(core * 8 + 1 + lo, n)]
        send(piece, piece, c2_s.at[i], c2_r.at[i], plane(dev_row))

    def plane_wait(i, q, lo=0, n=8):
        piece = xc.at[q, pl.ds(core * 8 + 1 + lo, n)]
        remote(piece, piece, c2_s.at[i], c2_r.at[i], plane(core_row)).wait_recv()

    def core_send(i, q):
        piece = xc.at[q, pl.ds(core * 8 + 1, 8)]
        send(piece, piece, cc_s.at[i], cc_r.at[i], plane(core_row))

    q_x, q_up, q_down = x_row // 2, yup_row // 2, ydown_row // 2
    q_xup, q_xdown = ((x_row + 4) % 16) // 2, ((x_row + 12) % 16) // 2
    q_opp, q_xopp = ((row + 8) % 16) // 2, ((x_row + 8) % 16) // 2

    own_quarter = pq.at[line, own]
    for i, (a, z) in enumerate(mates):
        send(own_quarter, own_quarter, gr_s.at[i], gr_r.at[i], {"ep": a, "row": row, "col": z})
    quarter_spread(0)
    for i in range(15):
        quarter_wait(i)
        quarter_spread(i + 1)
    block_stage(0, 0)
    other = (1 - ep) * 8 + col + 1
    remote(xr.at[other], xr.at[other], bx_s, bx_r, to_ep).wait_recv()
    for direction in range(2):
        ring_send(xr, xs, xq, direction, 0, 1)
    for z in range(8):
        piece = xc.at[q_own, core * 8 + z + 1]
        remote(piece, piece, c1_s.at[0], c1_r.at[z], plane(core_row)).wait_recv()
    plane_send(1, q_own, yup_row)
    plane_send(2, q_own, ydown_row)
    plane_send(0, q_own, x_row)
    for i in range(16):
        piece = pq.at[x_line, slots[i]]
        remote(piece, piece, px_s.at[i], px_r.at[i], plane(x_row)).wait_recv()
        send(piece, piece, pc_s.at[i], pc_r.at[i], plane(core_row))
    core_send(0, q_own)
    core_line = line + 1 - 2 * core
    for i in range(16):
        piece = pq.at[core_line, slots[i]]
        remote(piece, piece, po_s.at[i], po_r.at[i], plane(core_row)).wait_recv()
    core_line = (core_line + 2) % 4
    for i in range(16):
        piece = pq.at[core_line, slots[i]]
        remote(piece, piece, pc_s.at[i], pc_r.at[i], plane(core_row)).wait_recv()

    block_stage(1, 0)

    zero = jnp.zeros((EB, EB), BF16)

    def toeplitz_pair(e):
        first, second = (jnp.concatenate([pq[u, f + 1, EB:, :] for u in range(4)], axis=0) for f in (e, e + 1))
        return jnp.concatenate(
            [jnp.concatenate([first, zero], axis=1), jnp.concatenate([zero, second], axis=1)], axis=0
        )

    for e in range(0, NE, 2):
        panel = jnp.concatenate(
            [jnp.concatenate([pq[u, f, :EB, :] for f in (e, e + 1, e + 2)], axis=0) for u in range(4)], axis=1
        )
        pf[e * EB : (e + 2) * EB, :] = dot_nn(toeplitz_pair(e), panel).astype(BF16)
    for b in range(8):
        cut = slice(b * 128, (b + 1) * 128)
        pft[:, cut] = pf[cut, :].T
    smat[...] = dot_nn(pft[...], pf[...])
    di = lax.broadcasted_iota(jnp.int32, (PAN, PAN), 0)
    dj = lax.broadcasted_iota(jnp.int32, (PAN, PAN), 1)
    reg_diag = jnp.where(di == dj, reg_ref[...], 0.0)
    smat[...] = smat[...] + reg_diag
    wmat[...] = jnp.zeros((PAN, PAN), F32)

    def stage_a():
        plane_wait(1, q_down)
        plane_send(5, q_down, yup_row, 0, 4)
        plane_wait(2, q_up)
        plane_send(6, q_up, ydown_row, 4, 4)
        plane_wait(0, q_x)
        plane_send(3, q_x, yup_row)
        plane_send(4, q_x, ydown_row)
        core_send(1, q_x)
        core_send(2, q_down)
        core_send(3, q_up)

    def stage_b():
        block_stage(2, 0)

    def stage_c():
        plane_wait(3, q_xdown)
        plane_send(7, q_xdown, yup_row, 0, 4)
        core_send(4, q_xdown)
        plane_wait(4, q_xup)
        plane_send(8, q_xup, ydown_row, 4, 4)
        core_send(5, q_xup)

    def stage_d():
        block_stage(1, 1)

    def stage_e():
        block_stage(2, 1)

    def stage_f():
        plane_wait(5, q_opp, 0, 4)
        plane_wait(6, q_opp, 4, 4)
        core_send(6, q_opp)
        plane_wait(7, q_xopp, 0, 4)
        plane_wait(8, q_xopp, 4, 4)
        core_send(7, q_xopp)

    block_stage(0, 1)
    factor_step(smat, wmat, spread, 0, {7: stage_a, 15: stage_b})
    factor_step(smat, wmat, spread, 1, {3: stage_d, 9: stage_c})
    factor_step(smat, wmat, spread, 2, {3: stage_e, 15: stage_f})
    factor_step(smat, wmat, spread, 3)
    block_stage(3, 0)
    block_stage(3, 1)
    for i, q in enumerate((q_own, q_x, q_down, q_up, q_xdown, q_xup, q_opp, q_xopp)):
        piece = xc.at[q, pl.ds((1 - core) * 8 + 1, 8)]
        remote(piece, piece, cc_s.at[i], cc_r.at[i], plane(core_row)).wait_recv()

    for e in range(0, NE, 2):
        toep = toeplitz_pair(e)
        cut = slice(e * EB, (e + 2) * EB)
        frt_ref[:, cut] = dot_nn(toep, xr[e : e + 3].reshape(3 * EB, 1024)).astype(BF16).T
        columns = jnp.concatenate([xc[q, e : e + 3].reshape(3 * EB, PB) for q in range(8)], axis=1)
        fc_ref[cut, :] = dot_nn(toep, columns).astype(BF16)

    wh, wl = split2(wmat[...])

    def solve_weights(half):
        rows, depth = slice(half * HALF, (half + 1) * HALF), (half + 1) * HALF
        return jnp.concatenate([wh[rows, :depth], wl[rows, :depth], wh[rows, :depth]], axis=1)

    weights = [solve_weights(half) for half in range(2)]
    for b in range(2):
        cut = slice(b * PAN, (b + 1) * PAN)
        ar = dot_nn(frt_ref[cut, :], pf[...])
        if b == 0:
            ar = ar + jnp.where(row == 0, reg_diag, 0.0)
        ah, al = split2(ar)
        for half in range(2):
            depth = (half + 1) * HALF
            rr_ref[cut, half * HALF : depth] = dot_nt(
                jnp.concatenate([ah[:, :depth], ah[:, :depth], al[:, :depth]], axis=1), weights[half]
            )
        act = dot_nn(pft[...], fc_ref[:, cut])
        if b == 0:
            act = act + jnp.where(group == 0, reg_diag, 0.0)
        ah, al = split2(act)
        for half in range(2):
            depth = (half + 1) * HALF
            rct_ref[half * HALF : depth, cut] = dot_nn(
                weights[half], jnp.concatenate([ah[:depth], ah[:depth], al[:depth]], axis=0)
            )

    for copy in sends:
        copy.wait_send()
    for q in range(8):
        mine = jnp.logical_and(is_self, row // 2 == q)

        @pl.when(jnp.logical_not(mine))
        def _():
            remote(
                xr.at[own, :, q * PB : (q + 1) * PB], xc.at[q, own], c1_s.at[q], c1_r.at[col],
                {"ep": row // 8, "row": 2 * q + ep, "col": row % 8},
            ).wait_send()

    @pl.when(row == 0)
    def _():
        for t in range(1, 16):
            u = t % 4
            remote(
                xr.at[own, :, u * 128 : (u + 1) * 128], pq.at[u, own, 0:EB],
                p1_s.at[t - 1], p1_r, plane(t),
            ).wait_send()


def tile_kernel(frt_ref, fc_ref, rr_ref, rct_ref, reg_ref, out_ref, rcat):
    step = pl.program_id(0)
    rows_step = out_ref.shape[0]
    cols = out_ref.shape[1]
    row = lax.axis_index("row")
    group = lax.axis_index("ep") * 8 + lax.axis_index("col")

    @pl.when(step == 0)
    def _():
        rh, rl = split2(rct_ref[...])
        rcat[0:PAN] = rh
        rcat[PAN : 2 * PAN] = rl
        rcat[2 * PAN :] = rh

    base = row * 1024 + step * rows_step
    here = pl.ds(pl.multiple_of(step * rows_step, rows_step), rows_step)
    rr = rr_ref[here, :]
    ah, al = split2(rr)
    schur = dot_nn(jnp.concatenate([ah, ah, al], axis=1), rcat[...])
    tile = dot_nn(frt_ref[here, :], fc_ref[...])
    gr = base + lax.broadcasted_iota(jnp.int32, (rows_step, cols), 0)
    gc = group * 1024 + lax.broadcasted_iota(jnp.int32, (rows_step, cols), 1)
    reg = reg_ref[...]
    value = tile + jnp.where(gr == gc, reg, 0.0) - schur
    out_ref[...] = jnp.where(gr >= PAN, value, 0.0)

    @pl.when(group == 0)
    def _():
        pr = base + lax.broadcasted_iota(jnp.int32, (rows_step, PAN), 0)
        pc = lax.broadcasted_iota(jnp.int32, (rows_step, PAN), 1)
        out_ref[:, :PAN] = jnp.where(jnp.logical_and(pr < HALF, pc >= HALF), 0.0, rr)


def on_device(design, taps, tap_count, order, regular):
    vm = pl.BlockSpec(memory_space=pltpu.VMEM)
    dma = pltpu.SemaphoreType.DMA
    reg = regular.reshape(1, -1)
    frt, fc, rr, rct, regc = pl.pallas_call(
        gather_kernel,
        out_shape=(
            pltpu.VMEM((1024, 1024), BF16),
            pltpu.VMEM((1024, 1024), BF16),
            pltpu.VMEM((1024, PAN), F32),
            pltpu.VMEM((PAN, 1024), F32),
            pltpu.VMEM((1, 1024), F32),
        ),
        in_specs=[pl.BlockSpec(memory_space=pltpu.HBM)] * 5,
        out_specs=(vm, vm, vm, vm, vm),
        scratch_shapes=[
            pltpu.VMEM((NE + 1, EB, 1024), BF16),
            pltpu.VMEM((8, NE + 1, EB, PB), BF16),
            pltpu.VMEM((4, NE + 1, QR, 128), BF16),
            pltpu.VMEM((EB, 128), BF16),
            pltpu.VMEM((1024, PAN), BF16),
            pltpu.VMEM((PAN, 1024), BF16),
            pltpu.VMEM((PAN, PAN), F32),
            pltpu.VMEM((PAN, PAN), F32),
            pltpu.VMEM((144, 128), F32),
            pltpu.VMEM((EB, 1024), BF16),
            pltpu.SMEM((64,), F32),
            pltpu.VMEM((1, EB), jnp.int32),
            pltpu.VMEM((1, 1024), jnp.int32),
            pltpu.VMEM((1, PAN), F32),
            dma((6,)),
            dma, dma,
            dma((15,)), dma,
            dma((8,)), dma((8,)),
            dma((2, 4, 2)), dma((2, 4, 2)),
            dma((15,)), dma((15,)),
            dma((16,)), dma((16,)),
            dma((16,)), dma((16,)),
            dma((16,)), dma((16,)),
            dma((9,)), dma((9,)),
            dma((8,)), dma((8,)),
        ],
        compiler_params=pltpu.CompilerParams(
            collective_id=0, has_side_effects=True, vmem_limit_bytes=58450000
        ),
        name="gather",
    )(design, taps, tap_count.reshape(1, -1), order.reshape(1, -1), reg)
    rows_step = 256
    return pl.pallas_call(
        tile_kernel,
        grid=(1024 // rows_step,),
        out_shape=jax.ShapeDtypeStruct((1024, 1024), F32),
        in_specs=[
            vm, vm, vm, vm, vm,
        ],
        out_specs=pl.BlockSpec((rows_step, 1024), lambda i: (i, 0)),
        scratch_shapes=[pltpu.VMEM((3 * PAN, 1024), BF16)],
        compiler_params=pltpu.CompilerParams(vmem_limit_bytes=36 << 20),
        name="tile",
    )(frt, fc, rr, rct, regc)


def solution(mesh):
    in_specs = (P(("ep", "col"), "row"), P(), P(("ep", "col")), P("row"), P())
    out_specs = P("row", ("ep", "col"))
    return jax.shard_map(
        on_device, mesh=mesh, in_specs=in_specs, out_specs=out_specs, check_vma=False
    )
```

```python
import functools

import jax
import jax.numpy as jnp
from jax import lax
from jax.experimental import pallas as pl
from jax.experimental.pallas import tpu as pltpu
from jax.sharding import PartitionSpec as P

MESH = pl.DeviceIdType.MESH
F32 = jnp.float32
BF16 = jnp.bfloat16
HIGHEST = lax.Precision.HIGHEST
PB = 128
PAN = 512
EB = 64
NE = 16
HALF = 256
QR = EB + 16


def dot_nn(a, b, precision=None):
    return lax.dot_general(
        a, b, (((1,), (0,)), ((), ())), precision=precision, preferred_element_type=F32
    )


def dot_nt(a, b, precision=None):
    return lax.dot_general(
        a, b, (((1,), (1,)), ((), ())), precision=precision, preferred_element_type=F32
    )


def split2(x):
    high = x.astype(BF16)
    return high, (x - high.astype(F32)).astype(BF16)


def lane_bcast(v, j):
    return jnp.broadcast_to(v[:, j : j + 1], (8, 128))


def reciprocal(x):
    r = pl.reciprocal(x, approx=True)
    r = r * (2.0 - x * r)
    return r * (2.0 - x * r)


def invert_factor(groups, spread, hooks):
    sub = lax.broadcasted_iota(jnp.int32, (8, 128), 0)
    lane = lax.broadcasted_iota(jnp.int32, (8, 128), 1)
    a = list(groups)
    out = [None] * 16
    for p in range(16):
        base = (p % 2) * 72
        v = a[p]
        c = [lane_bcast(v, 8 * p + k) for k in range(8)]
        here = (lane >= 8 * p) & (lane < 8 * p + 8)
        m = jnp.where(here, jnp.where(lane - 8 * p == sub, 1.0, 0.0), v)
        for k in range(8):
            spread[base + 8 * k : base + 8 * k + 8, :] = c[k]
        spread[base + 64 : base + 72, :] = m
        s = [[None] * 8 for _ in range(8)]
        for k in range(8):
            for i in range(k, 8):
                s[i][k] = spread[pl.ds(base + 8 * k + i, 8, stride=0), :]
        rows = [spread[pl.ds(base + 64 + k, 8, stride=0), :] for k in range(8)]
        later = range(p + 1, 16)
        d = {q: [lane_bcast(a[q], 8 * p + k) for k in range(8)] for q in later}
        for q in later:
            a[q] = jnp.where(here, 0.0, a[q])
        for k in range(8):
            r = reciprocal(s[k][k])
            for i in range(k + 1, 8):
                w = s[i][k] * r
                for j in range(k + 1, i + 1):
                    s[i][j] = s[i][j] - w * s[j][k]
                rows[i] = rows[i] - w * rows[k]
            for q in later:
                w = d[q][k] * r
                for i in range(k + 1, 8):
                    d[q][i] = d[q][i] - w * s[i][k]
                a[q] = a[q] - w * rows[k]
        done = rows[0] * lax.rsqrt(s[0][0])
        for k in range(1, 8):
            done = jnp.where(sub == k, rows[k] * lax.rsqrt(s[k][k]), done)
        out[p] = jnp.where(lane < 8 * p + 8, done, 0.0)
        if p in hooks:
            hooks[p]()
    return out


def factor_step(s, w, spread, b, hooks={}):
    n = s.shape[0]
    lo, hi = 128 * b, 128 * b + 128
    g = invert_factor([s[lo + 8 * q : lo + 8 * q + 8, lo:hi] for q in range(16)], spread, hooks)
    for q in range(16):
        w[lo + 8 * q : lo + 8 * q + 8, lo:hi] = g[q]
    inv = w[lo:hi, lo:hi]
    if b > 0:
        w[lo:hi, :lo] = dot_nn(inv, w[lo:hi, :lo], HIGHEST)
    if hi < n:
        below = dot_nt(s[hi:, lo:hi], inv, HIGHEST)
        s[hi:, hi:] = s[hi:, hi:] - dot_nt(below, below, HIGHEST)
        w[hi:, :hi] = w[hi:, :hi] - dot_nn(below, w[lo:hi, :hi], HIGHEST)


def gather_kernel(
    design_in, taps_in, count_in, order_in, reg_in,
    frt_ref, fc_ref, rr_ref, rct_ref, regc_ref,
    xr, xc, pq, band_ref, pf, pft, smat, wmat, spread,
    design_ref, taps_ref, count_ref, order_ref, reg_ref,
    in_s, bx_s, bx_r, p1_s, p1_r, c1_s, c1_r, xs, xq, gr_s, gr_r, px_s, px_r, po_s, po_r, pc_s, pc_r,
    c2_s, c2_r, cc_s, cc_r,
):
    group = lax.axis_index("ep") * 8 + lax.axis_index("col")
    loads = [
        pltpu.make_async_copy(order_in, order_ref, in_s.at[0]),
        pltpu.make_async_copy(design_in, design_ref, in_s.at[1]),
        pltpu.make_async_copy(taps_in, taps_ref, in_s.at[2]),
        pltpu.make_async_copy(count_in, count_ref, in_s.at[3]),
        pltpu.make_async_copy(reg_in.at[:, pl.ds(0, PAN)], reg_ref, in_s.at[4]),
        pltpu.make_async_copy(
            reg_in.at[:, pl.ds(pl.multiple_of(group * 1024, 1024), 1024)], regc_ref, in_s.at[5]
        ),
    ]
    for load in loads:
        load.start()
    ep = lax.axis_index("ep")
    row = lax.axis_index("row")
    col = lax.axis_index("col")
    core = row % 2
    e_own = ep * 8 + col
    line = row % 4
    up, down = (col + 1) % 8, (col + 7) % 8
    to_up = {"ep": ep, "row": row, "col": up}
    to_down = {"ep": ep, "row": row, "col": down}
    to_ep = {"ep": 1 - ep, "row": row, "col": col}
    core_row = row - core + (1 - core)
    xlo = (row // 2) % 2
    x_row = row + 2 - 4 * xlo
    yup_row, ydown_row = (row + 4) % 16, (row + 12) % 16
    plane = lambda r: {"ep": ep, "row": r, "col": col}
    is_self = jnp.logical_and(row == group, core == ep)

    barrier = pltpu.get_barrier_semaphore()
    for dev in (plane(core_row), plane(x_row), plane(yup_row), plane(ydown_row)):
        pl.semaphore_signal(barrier, inc=1, device_id=dev, device_id_type=MESH)
    mates = []
    for dz, de in ((1, 0), (7, 0), (0, 1), (2, 0), (6, 0), (1, 1), (7, 1), (3, 0), (5, 0), (2, 1), (6, 1), (4, 0), (3, 1), (5, 1), (4, 1)):
        mate_ep, mate_col = (ep + de) % 2, (col + dz) % 8
        mates.append((mate_ep, mate_col))
        pl.semaphore_signal(
            barrier, inc=1, device_id={"ep": mate_ep, "row": row, "col": mate_col}, device_id_type=MESH
        )

    @pl.when(row != 0)
    def _():
        pl.semaphore_signal(barrier, inc=1, device_id=plane(0), device_id_type=MESH)

    for z in range(8):
        mine = jnp.logical_and(is_self, col == z)

        @pl.when(jnp.logical_not(mine))
        def _():
            pl.semaphore_signal(
                barrier, inc=1, device_id={"ep": core, "row": group, "col": z}, device_id_type=MESH
            )

    for load in loads:
        load.wait()
    local = order_ref[...] % PB
    kk = lax.broadcasted_iota(jnp.int32, (PB, 1024), 0)
    one_hot = jnp.where(kk == local, 1.0, 0.0).astype(BF16)
    own = e_own + 1
    for g in range(8):
        part = dot_nn(design_ref[:, g * PB : (g + 1) * PB], one_hot[:, g * PB : (g + 1) * PB])
        xr[own, :, g * PB : (g + 1) * PB] = part.astype(BF16)
    ii = lax.broadcasted_iota(jnp.int32, (EB, 128), 0)
    jj = lax.broadcasted_iota(jnp.int32, (EB, 128), 1)
    lag = ii + EB - jj
    ti = lax.broadcasted_iota(jnp.int32, (EB, EB), 0)
    tj = lax.broadcasted_iota(jnp.int32, (EB, EB), 1)
    counts = jnp.sum(jnp.where(ti == tj, count_ref[...].astype(F32), 0.0), axis=1, keepdims=True)
    band = jnp.zeros((EB, 128), F32)
    for t in range(taps_ref.shape[0]):
        band = jnp.where(lag == t, taps_ref[t], band)
    band = jnp.where(lag.astype(F32) < counts, band, 0.0)
    band_ref[...] = band.astype(BF16)
    pq[line, own, EB:, :] = band_ref[pl.ds(pl.multiple_of(16 * line, 16), 16), :]
    xr[0] = jnp.zeros(xr.shape[1:], BF16)
    for u in range(4):
        pq[u, 0] = jnp.zeros((QR, 128), BF16)
    for q in range(8):
        xc[q, 0] = jnp.zeros((EB, PB), BF16)

    @pl.when(row == 0)
    def _():
        pq[0, own, :EB, :] = xr[own, :, :128]

    pl.semaphore_wait(
        barrier, 4 + 15 + 8 + jnp.where(row == 0, 15, 0) - jnp.where(is_self, 1, 0)
    )

    sends = []

    def remote(src, dst, s_sem, r_sem, dev):
        return pltpu.make_async_remote_copy(
            src_ref=src, dst_ref=dst, send_sem=s_sem, recv_sem=r_sem, device_id=dev, device_id_type=MESH
        )

    def send(src, dst, s_sem, r_sem, dev):
        copy = remote(src, dst, s_sem, r_sem, dev)
        copy.start()
        sends.append(copy)

    @pl.when(row == 0)
    def _():
        for t in range(1, 16):
            u = t % 4
            remote(
                xr.at[own, :, u * 128 : (u + 1) * 128], pq.at[u, own, 0:EB],
                p1_s.at[t - 1], p1_r, plane(t),
            ).start()

    eps = (ep, 1 - ep)

    def ring_origin(direction, s):
        return (col + 8 - s) % 8 if direction == 0 else (col + s) % 8

    def ring_piece(buf, k, z, direction, s):
        slot = eps[k] * 8 + z + 1
        if s < 3:
            return buf.at[slot]
        return buf.at[slot, pl.ds(32 * direction, 32)]

    def ring_send(buf, ssem, rsem, direction, s, k):
        piece = ring_piece(buf, k, ring_origin(direction, s), direction, s)
        send(piece, piece, ssem.at[direction, s, k], rsem.at[direction, s, k], (to_up, to_down)[direction])

    def ring_wait(buf, ssem, rsem, direction, s, k):
        piece = ring_piece(buf, k, ring_origin(direction, s + 1), direction, s)
        remote(piece, piece, ssem.at[direction, s, k], rsem.at[direction, s, k], to_up).wait_recv()

    for direction in range(2):
        ring_send(xr, xs, xq, direction, 0, 0)
    @pl.when(row != 0)
    def _():
        piece = pq.at[line, own, 0:EB]
        remote(piece, piece, p1_s.at[0], p1_r, plane(0)).wait_recv()

    x_line = (line + 2) % 4
    back = (1, 0, 2, 4, 3, 6, 5, 8, 7, 10, 9, 11, 13, 12, 14)
    slots = [own] + [a * 8 + z + 1 for a, z in mates]

    def quarter_spread(i):
        piece = pq.at[line, slots[i]]
        send(piece, piece, px_s.at[i], px_r.at[i], plane(x_row))
        send(piece, piece, po_s.at[i], po_r.at[i], plane(core_row))

    def quarter_wait(i):
        piece = pq.at[line, slots[i + 1]]
        remote(piece, piece, gr_s.at[i], gr_r.at[back[i]], to_up).wait_recv()

    def block_stage(s, k):
        for direction in range(2):
            ring_wait(xr, xs, xq, direction, s, k)
            if s < 3:
                ring_send(xr, xs, xq, direction, s + 1, k)

    q_own = row // 2

    def plane_send(i, q, dev_row, lo=0, n=8):
        piece = xc.at[q, pl.ds(core * 8 + 1 + lo, n)]
        send(piece, piece, c2_s.at[i], c2_r.at[i], plane(dev_row))

    def plane_wait(i, q, lo=0, n=8):
        piece = xc.at[q, pl.ds(core * 8 + 1 + lo, n)]
        remote(piece, piece, c2_s.at[i], c2_r.at[i], plane(core_row)).wait_recv()

    def core_send(i, q):
        piece = xc.at[q, pl.ds(core * 8 + 1, 8)]
        send(piece, piece, cc_s.at[i], cc_r.at[i], plane(core_row))

    q_x, q_up, q_down = x_row // 2, yup_row // 2, ydown_row // 2
    q_xup, q_xdown = ((x_row + 4) % 16) // 2, ((x_row + 12) % 16) // 2
    q_opp, q_xopp = ((row + 8) % 16) // 2, ((x_row + 8) % 16) // 2

    own_quarter = pq.at[line, own]
    for i, (a, z) in enumerate(mates):
        send(own_quarter, own_quarter, gr_s.at[i], gr_r.at[i], {"ep": a, "row": row, "col": z})
    quarter_spread(0)
    for q in range(8):
        src = xr.at[own, :, q * PB : (q + 1) * PB]
        dst = xc.at[q, own]
        mine = jnp.logical_and(is_self, row // 2 == q)

        @pl.when(jnp.logical_not(mine))
        def _():
            remote(
                src, dst, c1_s.at[q], c1_r.at[col],
                {"ep": row // 8, "row": 2 * q + ep, "col": row % 8},
            ).start()

        @pl.when(mine)
        def _():
            pltpu.make_async_copy(src, dst, c1_r.at[col]).start()

    send(xr.at[own], xr.at[own], bx_s, bx_r, to_ep)
    for i in range(15):
        quarter_wait(i)
        quarter_spread(i + 1)
    block_stage(0, 0)
    other = (1 - ep) * 8 + col + 1
    remote(xr.at[other], xr.at[other], bx_s, bx_r, to_ep).wait_recv()
    for direction in range(2):
        ring_send(xr, xs, xq, direction, 0, 1)
    for z in range(8):
        piece = xc.at[q_own, core * 8 + z + 1]
        remote(piece, piece, c1_s.at[0], c1_r.at[z], plane(core_row)).wait_recv()
    plane_send(1, q_own, yup_row)
    plane_send(2, q_own, ydown_row)
    plane_send(0, q_own, x_row)
    for i in range(16):
        piece = pq.at[x_line, slots[i]]
        remote(piece, piece, px_s.at[i], px_r.at[i], plane(x_row)).wait_recv()
        send(piece, piece, pc_s.at[i], pc_r.at[i], plane(core_row))
    core_send(0, q_own)
    core_line = line + 1 - 2 * core
    for i in range(16):
        piece = pq.at[core_line, slots[i]]
        remote(piece, piece, po_s.at[i], po_r.at[i], plane(core_row)).wait_recv()
    core_line = (core_line + 2) % 4
    for i in range(16):
        piece = pq.at[core_line, slots[i]]
        remote(piece, piece, pc_s.at[i], pc_r.at[i], plane(core_row)).wait_recv()

    block_stage(1, 0)

    zero = jnp.zeros((EB, EB), BF16)

    def toeplitz_pair(e):
        first, second = (jnp.concatenate([pq[u, f + 1, EB:, :] for u in range(4)], axis=0) for f in (e, e + 1))
        return jnp.concatenate(
            [jnp.concatenate([first, zero], axis=1), jnp.concatenate([zero, second], axis=1)], axis=0
        )

    for e in range(0, NE, 2):
        panel = jnp.concatenate(
            [jnp.concatenate([pq[u, f, :EB, :] for f in (e, e + 1, e + 2)], axis=0) for u in range(4)], axis=1
        )
        pf[e * EB : (e + 2) * EB, :] = dot_nn(toeplitz_pair(e), panel).astype(BF16)
    for b in range(8):
        cut = slice(b * 128, (b + 1) * 128)
        pft[:, cut] = pf[cut, :].T
    smat[...] = dot_nn(pft[...], pf[...])
    di = lax.broadcasted_iota(jnp.int32, (PAN, PAN), 0)
    dj = lax.broadcasted_iota(jnp.int32, (PAN, PAN), 1)
    reg_diag = jnp.where(di == dj, reg_ref[...], 0.0)
    smat[...] = smat[...] + reg_diag
    wmat[...] = jnp.zeros((PAN, PAN), F32)

    def stage_a():
        plane_wait(1, q_down)
        plane_send(5, q_down, yup_row, 0, 4)
        plane_wait(2, q_up)
        plane_send(6, q_up, ydown_row, 4, 4)
        plane_wait(0, q_x)
        plane_send(3, q_x, yup_row)
        plane_send(4, q_x, ydown_row)
        core_send(1, q_x)
        core_send(2, q_down)
        core_send(3, q_up)

    def stage_b():
        block_stage(2, 0)

    def stage_c():
        plane_wait(3, q_xdown)
        plane_send(7, q_xdown, yup_row, 0, 4)
        core_send(4, q_xdown)
        plane_wait(4, q_xup)
        plane_send(8, q_xup, ydown_row, 4, 4)
        core_send(5, q_xup)

    def stage_d():
        block_stage(1, 1)

    def stage_e():
        block_stage(2, 1)

    def stage_f():
        plane_wait(5, q_opp, 0, 4)
        plane_wait(6, q_opp, 4, 4)
        core_send(6, q_opp)
        plane_wait(7, q_xopp, 0, 4)
        plane_wait(8, q_xopp, 4, 4)
        core_send(7, q_xopp)

    block_stage(0, 1)
    factor_step(smat, wmat, spread, 0, {7: stage_a, 15: stage_b})
    factor_step(smat, wmat, spread, 1, {3: stage_d, 9: stage_c})
    factor_step(smat, wmat, spread, 2, {3: stage_e, 15: stage_f})
    factor_step(smat, wmat, spread, 3)
    block_stage(3, 0)
    block_stage(3, 1)
    for i, q in enumerate((q_own, q_x, q_down, q_up, q_xdown, q_xup, q_opp, q_xopp)):
        piece = xc.at[q, pl.ds((1 - core) * 8 + 1, 8)]
        remote(piece, piece, cc_s.at[i], cc_r.at[i], plane(core_row)).wait_recv()

    for e in range(0, NE, 2):
        toep = toeplitz_pair(e)
        cut = slice(e * EB, (e + 2) * EB)
        frt_ref[:, cut] = dot_nn(toep, xr[e : e + 3].reshape(3 * EB, 1024)).astype(BF16).T
        columns = jnp.concatenate([xc[q, e : e + 3].reshape(3 * EB, PB) for q in range(8)], axis=1)
        fc_ref[cut, :] = dot_nn(toep, columns).astype(BF16)

    wh, wl = split2(wmat[...])

    def solve_weights(half):
        rows, depth = slice(half * HALF, (half + 1) * HALF), (half + 1) * HALF
        return jnp.concatenate([wh[rows, :depth], wl[rows, :depth], wh[rows, :depth]], axis=1)

    weights = [solve_weights(half) for half in range(2)]
    for b in range(2):
        cut = slice(b * PAN, (b + 1) * PAN)
        ar = dot_nn(frt_ref[cut, :], pf[...])
        if b == 0:
            ar = ar + jnp.where(row == 0, reg_diag, 0.0)
        ah, al = split2(ar)
        for half in range(2):
            depth = (half + 1) * HALF
            rr_ref[cut, half * HALF : depth] = dot_nt(
                jnp.concatenate([ah[:, :depth], ah[:, :depth], al[:, :depth]], axis=1), weights[half]
            )
        act = dot_nn(pft[...], fc_ref[:, cut])
        if b == 0:
            act = act + jnp.where(group == 0, reg_diag, 0.0)
        ah, al = split2(act)
        for half in range(2):
            depth = (half + 1) * HALF
            rct_ref[half * HALF : depth, cut] = dot_nn(
                weights[half], jnp.concatenate([ah[:depth], ah[:depth], al[:depth]], axis=0)
            )

    for copy in sends:
        copy.wait_send()
    for q in range(8):
        mine = jnp.logical_and(is_self, row // 2 == q)

        @pl.when(jnp.logical_not(mine))
        def _():
            remote(
                xr.at[own, :, q * PB : (q + 1) * PB], xc.at[q, own], c1_s.at[q], c1_r.at[col],
                {"ep": row // 8, "row": 2 * q + ep, "col": row % 8},
            ).wait_send()

    @pl.when(row == 0)
    def _():
        for t in range(1, 16):
            u = t % 4
            remote(
                xr.at[own, :, u * 128 : (u + 1) * 128], pq.at[u, own, 0:EB],
                p1_s.at[t - 1], p1_r, plane(t),
            ).wait_send()


def tile_kernel(frt_ref, fc_ref, rr_ref, rct_ref, reg_ref, out_ref, rcat):
    step = pl.program_id(0)
    rows_step = out_ref.shape[0]
    cols = out_ref.shape[1]
    row = lax.axis_index("row")
    group = lax.axis_index("ep") * 8 + lax.axis_index("col")

    @pl.when(step == 0)
    def _():
        rh, rl = split2(rct_ref[...])
        rcat[0:PAN] = rh
        rcat[PAN : 2 * PAN] = rl
        rcat[2 * PAN :] = rh

    base = row * 1024 + step * rows_step
    here = pl.ds(pl.multiple_of(step * rows_step, rows_step), rows_step)
    rr = rr_ref[here, :]
    ah, al = split2(rr)
    schur = dot_nn(jnp.concatenate([ah, ah, al], axis=1), rcat[...])
    tile = dot_nn(frt_ref[here, :], fc_ref[...])
    gr = base + lax.broadcasted_iota(jnp.int32, (rows_step, cols), 0)
    gc = group * 1024 + lax.broadcasted_iota(jnp.int32, (rows_step, cols), 1)
    reg = reg_ref[...]
    value = tile + jnp.where(gr == gc, reg, 0.0) - schur
    out_ref[...] = jnp.where(gr >= PAN, value, 0.0)

    @pl.when(group == 0)
    def _():
        pr = base + lax.broadcasted_iota(jnp.int32, (rows_step, PAN), 0)
        pc = lax.broadcasted_iota(jnp.int32, (rows_step, PAN), 1)
        out_ref[:, :PAN] = jnp.where(jnp.logical_and(pr < HALF, pc >= HALF), 0.0, rr)


def on_device(design, taps, tap_count, order, regular):
    vm = pl.BlockSpec(memory_space=pltpu.VMEM)
    dma = pltpu.SemaphoreType.DMA
    reg = regular.reshape(1, -1)
    frt, fc, rr, rct, regc = pl.pallas_call(
        gather_kernel,
        out_shape=(
            pltpu.VMEM((1024, 1024), BF16),
            pltpu.VMEM((1024, 1024), BF16),
            pltpu.VMEM((1024, PAN), F32),
            pltpu.VMEM((PAN, 1024), F32),
            pltpu.VMEM((1, 1024), F32),
        ),
        in_specs=[pl.BlockSpec(memory_space=pltpu.HBM)] * 5,
        out_specs=(vm, vm, vm, vm, vm),
        scratch_shapes=[
            pltpu.VMEM((NE + 1, EB, 1024), BF16),
            pltpu.VMEM((8, NE + 1, EB, PB), BF16),
            pltpu.VMEM((4, NE + 1, QR, 128), BF16),
            pltpu.VMEM((EB, 128), BF16),
            pltpu.VMEM((1024, PAN), BF16),
            pltpu.VMEM((PAN, 1024), BF16),
            pltpu.VMEM((PAN, PAN), F32),
            pltpu.VMEM((PAN, PAN), F32),
            pltpu.VMEM((144, 128), F32),
            pltpu.VMEM((EB, 1024), BF16),
            pltpu.SMEM((64,), F32),
            pltpu.VMEM((1, EB), jnp.int32),
            pltpu.VMEM((1, 1024), jnp.int32),
            pltpu.VMEM((1, PAN), F32),
            dma((6,)),
            dma, dma,
            dma((15,)), dma,
            dma((8,)), dma((8,)),
            dma((2, 4, 2)), dma((2, 4, 2)),
            dma((15,)), dma((15,)),
            dma((16,)), dma((16,)),
            dma((16,)), dma((16,)),
            dma((16,)), dma((16,)),
            dma((9,)), dma((9,)),
            dma((8,)), dma((8,)),
        ],
        compiler_params=pltpu.CompilerParams(
            collective_id=0, has_side_effects=True, vmem_limit_bytes=58450000
        ),
        name="gather",
    )(design, taps, tap_count.reshape(1, -1), order.reshape(1, -1), reg)
    rows_step = 256
    return pl.pallas_call(
        tile_kernel,
        grid=(1024 // rows_step,),
        out_shape=jax.ShapeDtypeStruct((1024, 1024), F32),
        in_specs=[
            vm, vm, vm, vm, vm,
        ],
        out_specs=pl.BlockSpec((rows_step, 1024), lambda i: (i, 0)),
        scratch_shapes=[pltpu.VMEM((3 * PAN, 1024), BF16)],
        compiler_params=pltpu.CompilerParams(vmem_limit_bytes=36 << 20),
        name="tile",
    )(frt, fc, rr, rct, regc)


def solution(mesh):
    in_specs = (P(("ep", "col"), "row"), P(), P(("ep", "col")), P("row"), P())
    out_specs = P("row", ("ep", "col"))
    return jax.shard_map(
        on_device, mesh=mesh, in_specs=in_specs, out_specs=out_specs, check_vma=False
    )
```
